256 devices in a mesh: vehicle: 4 (over y), track: 16 (over x, z_lo, core), cross: 4 (over z_hi).
Axes of the slice: x: 4, y: 4, z: 8 (z_hi: 4, z_lo: 2; z = z_hi * 2 + z_lo), core: 2. Of those that a mesh axis runs over, the one named last changes fastest.
Arguments:
- particle_offset: float32 [3, 128, 32, 128], P(None, ('vehicle', 'track'), 'cross'), may hold values from 0 to 1
- particle_velocity: float32 [3, 128, 32, 128], P(None, ('vehicle', 'track'), 'cross'), may hold values from -4 to 4
- cell_count: int32 [128, 32], P(('vehicle', 'track'), 'cross'), may hold values from 32 to 128
- face_offset: float32 [16384, 3, 128], P(('vehicle', 'track', 'cross')), may hold values from 0 to 1
- face_velocity: float32 [16384, 3, 128], P(('vehicle', 'track', 'cross')), may hold values from -4 to 4
- face_route: int32 [16384, 1], P(('vehicle', 'track', 'cross')), may hold values from 0 to 63; in each aligned block of 64 rows (0 to 63, 64 to 127, ...) at most 4 rows name the same one
- face_cell: int32 [16384], P(('vehicle', 'track', 'cross')), may hold values from 0 to 15
Outputs:
- moved_offset: float32 [3, 128, 32, 128], P(None, ('vehicle', 'track'), 'cross')
- new_velocity: float32 [3, 128, 32, 128], P(None, ('vehicle', 'track'), 'cross')
- face_impulse: float32 [16384, 3, 128], P(('vehicle', 'track', 'cross'))
The draws below stay inside these ranges and needn't reach their ends.
Inputs may be any that keep to these rules, and one draw needn't show every extreme that they name: `face_route`: among the 64 face blocks of one owner device, at most 4 name the same terrain device, and that many is reached.
All inputs are finite; a program needn't handle non-finite values.
Results may differ from the reference program's by a relative error of at most 0.0003.
Values sent between devices are 32-bit elements; how exact they have to be, the bound alone decides.
A program may use at most 64 MiB of HBM per device.

```python
import math
import jax
import jax.numpy as jnp
import numpy as np
from jax import lax

CT = 2
CC = 8
SLOTS = 128
FACES = 128
FB_DEV = 64
CAP = 4
ROWS_T = 128
ROWS_C = 32
FBLOCKS = 16384
N_TRACK = 16
N_CROSS = 4


def set_ends(drawn, key, low, high):
    index_at = [jax.random.randint(jax.random.fold_in(key, axis), (), 0, length) for axis, length in enumerate(drawn.shape)]
    main_axis = drawn.shape.index(max(drawn.shape))
    beside = index_at[:main_axis] + [(index_at[main_axis] + 1) % drawn.shape[main_axis]] + index_at[main_axis + 1:]
    return drawn.at[tuple(index_at)].set(low).at[tuple(beside)].set(high)


def level_of(rng, shape, cuts, low, high):
    def one(dim, parts):
        heights = jax.random.uniform(jax.random.fold_in(jax.random.fold_in(rng, 6), dim), (parts,), jnp.float32, low / len(cuts), high / len(cuts))
        return jnp.repeat(jnp.exp(heights), shape[dim] // parts).reshape((-1,) + (1,) * (len(shape) - dim - 1))

    level = one(*cuts[0])
    for cut in cuts[1:]:
        level = level * one(*cut)
    return level


def routed_block(own_key, own, number, rows, number_of, top, bound, slope):
    sequence = jax.random.permutation(own_key, number_of)
    heavy_load, common = shares(number_of, rows * top, bound, slope, True), shares(number_of, rows * top, bound, slope, False)
    places = jnp.arange(number_of)

    def named(lengths, turn):
        used = int((lengths > 0).sum())
        fixed = max(1, used // 4)
        passed = fixed + (places - fixed + turn * (used - fixed)) % max(1, number_of - fixed)
        return jnp.zeros((number_of,), jnp.int32).at[sequence[jnp.where(places < fixed, places, passed)]].set(jnp.asarray(lengths, jnp.int32))

    lengths = jnp.where(number % 4 == 0, named(heavy_load, number // 4), named(common, number - number // 4 - 1))
    mixed = jax.random.permutation(jax.random.fold_in(own, 3), number_of)
    source_of, receiver = mixed[0:number_of // 2 * 2:2], mixed[1:number_of // 2 * 2:2]
    slack = jnp.minimum(lengths[source_of] - 1, bound - lengths[receiver]) // 2
    slack = jnp.where((source_of == sequence[0]) | (receiver == sequence[0]) | (lengths[receiver] == 0), 0, jnp.maximum(slack, 0))
    passed = jax.random.randint(jax.random.fold_in(own, 4), (number_of // 2,), 0, 1 << 20) % (slack + 1)
    lengths = lengths.at[source_of].add(-passed).at[receiver].add(passed)
    labels = jnp.searchsorted(jnp.cumsum(lengths), jnp.arange(rows * top), side="right").astype(jnp.int32)
    listing = labels.reshape(top, rows).T
    listing = listing[jax.random.permutation(jax.random.fold_in(own, 1), rows)]
    turn = jax.random.randint(jax.random.fold_in(own, 2), (rows, 1), 0, top)
    return jnp.take_along_axis(listing, (jnp.arange(top)[None, :] + turn) % top, axis=1)


def shares(amount, total, bound, skew, full):
    portions = [(1 << 20) // math.isqrt(rank ** skew) + 1 for rank in range(1, amount + 1)]
    largest = bound if full else min(bound, max(-(-total // amount), total * portions[0] // sum(portions)))
    least = 1 if total - largest >= amount - 1 else 0
    holding, surplus = [largest] + [least] * (amount - 1), total - largest - least * (amount - 1)
    while surplus > 0:
        free = [i for i in range(1, amount) if holding[i] < largest] or [i for i in range(1, amount) if holding[i] < bound]
        pool, remaining = sum([portions[i] for i in free]), surplus
        for i in free:
            addition = min(bound - holding[i], max(1, remaining * portions[i] // pool), surplus)
            holding[i] = holding[i] + addition
            surplus = surplus - addition
    return np.array(holding)


def centred(rng, dims, scale, most, cuts=(), held_as=jnp.bfloat16):
    entries = scale * jax.random.normal(rng, dims, jnp.float32)
    if cuts:
        entries = entries * level_of(rng, dims, cuts, -0.22, 0.18)
    return jnp.clip(entries, -most, most).astype(held_as)


def setup_inputs(seed: int = 0) -> dict:
    splits = jax.random.split(jax.random.key(seed), 8)
    particle_offset = jnp.clip(1.0 * jax.random.uniform(splits[0], (3, ROWS_T, ROWS_C, SLOTS), jnp.float32) ** level_of(splits[0], (3, ROWS_T, ROWS_C, SLOTS), ((1, 64), (2, 4)), -0.2, 0.2), 0.0, 1.0)
    particle_velocity = centred(splits[1], (3, ROWS_T, ROWS_C, SLOTS), 1.0, 4.0, ((1, 64), (2, 4)), jnp.float32)
    cell_count = set_ends(jax.random.randint(splits[2], (ROWS_T, ROWS_C), SLOTS // 4, SLOTS + 1), jax.random.fold_in(splits[2], 1), SLOTS // 4, SLOTS).astype(jnp.int32)
    face_offset = jnp.clip(1.0 * jax.random.uniform(splits[3], (FBLOCKS, 3, FACES), jnp.float32) ** level_of(splits[3], (FBLOCKS, 3, FACES), ((0, 256),), -0.2, 0.2), 0.0, 1.0)
    face_velocity = centred(splits[4], (FBLOCKS, 3, FACES), 1.0, 4.0, ((0, 256),), jnp.float32)
    face_route_keys = jax.random.split(jax.random.fold_in(splits[5], 1), FBLOCKS // FB_DEV)
    face_route_turns = jax.random.permutation(jax.random.fold_in(splits[5], 3), FBLOCKS // FB_DEV)
    face_route = jax.vmap(lambda own, number: routed_block(jax.random.fold_in(splits[5], 2), own, number, FB_DEV, N_TRACK * N_CROSS, 1, CAP, 2))(face_route_keys, face_route_turns).reshape((FBLOCKS, 1))
    face_cell = set_ends(jax.random.randint(splits[6], (FBLOCKS,), 0, CT * CC), jax.random.fold_in(splits[6], 1), 0, (CT * CC) - 1).astype(jnp.int32)
    return {"particle_offset": particle_offset, "particle_velocity": particle_velocity, "cell_count": cell_count, "face_offset": face_offset, "face_velocity": face_velocity, "face_route": face_route, "face_cell": face_cell}


radius = 0.1
face_radius = 0.15
stiffness = 100.0
damping = 40.0
soften = 0.05
time_step = 0.02
gravity = 9.81

def contact(own_pos, own_vel, other_pos, other_vel, other_live, reach):
    apart = own_pos[:, :, :, None] - other_pos[:, :, None, :]
    distance = jnp.sqrt(lax.optimization_barrier(jnp.sum(apart * apart, axis=0)) + soften * soften)
    normal = apart / distance[None]
    closing = lax.optimization_barrier(jnp.sum((own_vel[:, :, :, None] - other_vel[:, :, None, :]) * normal, axis=0))
    intersection = jnp.maximum(reach - distance, 0.0)
    weight = intersection * (stiffness - damping * closing) * other_live[:, None, :]
    return weight[None] * normal

def particle_forces(stacked, padded):
    across = stacked.shape[2]
    slot_count = stacked.shape[3]
    others = 1.0 - jnp.eye(slot_count, dtype=jnp.float32)

    def row_force(row_index):
        own_part = lax.dynamic_slice_in_dim(stacked, row_index, 1, 1)[:, 0]
        total_force = jnp.zeros((3, across, slot_count), jnp.float32)
        for shift_t in (-1, 0, 1):
            band_rows = lax.dynamic_slice_in_dim(padded, row_index + 1 + shift_t, 1, 1)[:, 0]
            for shift_c in (-1, 0, 1):
                neighbour = band_rows[:, 1 + shift_c:1 + shift_c + across]
                offset = jnp.array([shift_t, shift_c, 0.0], jnp.float32)[:, None, None]
                pushes = contact(own_part[0:3], own_part[3:6], neighbour[0:3] + offset, neighbour[3:6], neighbour[6], 2.0 * radius)
                if shift_t == 0 and shift_c == 0:
                    pushes = pushes * others
                total_force = total_force + lax.optimization_barrier(jnp.sum(pushes, axis=3))
        return total_force * own_part[6][None]
    forces = lax.map(row_force, jnp.arange(stacked.shape[1], dtype=jnp.int32))
    return jnp.transpose(forces, (1, 0, 2, 3))

def tire_contact(chosen, face_pos, face_vel):
    ones_live = jnp.ones((face_pos.shape[1], face_pos.shape[2]), jnp.float32)
    pushes = contact(chosen[0:3], chosen[3:6], face_pos, face_vel, ones_live, radius + face_radius)
    pushes = pushes * chosen[6][None, :, :, None]
    return (lax.optimization_barrier(jnp.sum(pushes, axis=3)), -lax.optimization_barrier(jnp.sum(pushes, axis=2)))

def reference(particle_offset, particle_velocity, cell_count, face_offset, face_velocity, face_route, face_cell):
    travel_rows, cross_rows, slot_count = particle_offset.shape[1:]
    faces = face_offset.shape[2]
    live = (lax.broadcasted_iota(jnp.int32, (travel_rows, cross_rows, slot_count), 2) < cell_count[:, :, None]).astype(jnp.float32)
    owners = jnp.arange(FBLOCKS, dtype=jnp.int32) // FB_DEV
    vehicle_index = owners // (N_TRACK * N_CROSS)
    target = face_route[:, 0]
    block_t = (vehicle_index * N_TRACK + target // N_CROSS) * CT + face_cell // CC
    block_c = target % N_CROSS * CC + face_cell % CC
    fall = jnp.array([0.0, 0.0, -gravity], jnp.float32)[:, None, None, None]
    groups = FBLOCKS // FB_DEV
    offsets = particle_offset
    velocity = particle_velocity
    reaction = jnp.zeros((FBLOCKS, 3, faces), jnp.float32)
    vel_spans = jnp.transpose(face_velocity.reshape(groups, FB_DEV, 3, faces), (0, 2, 1, 3))
    for substep in range(2):
        stacked = jnp.concatenate([offsets, velocity, live[None]], axis=0)
        padded = jnp.pad(stacked, ((0, 0), (1, 1), (1, 1), (0, 0)))
        total_push = particle_forces(stacked, padded)
        chosen = stacked[:, block_t, block_c, :]
        chosen_spans = jnp.transpose(chosen.reshape(7, groups, FB_DEV, slot_count), (1, 0, 2, 3))
        faces_now = face_offset + substep * time_step * face_velocity
        pos_spans = jnp.transpose(faces_now.reshape(groups, FB_DEV, 3, faces), (0, 2, 1, 3))

        def face_group(pieces):
            return tire_contact(pieces[0], pieces[1], pieces[2])
        on_particles, on_faces = lax.map(face_group, (chosen_spans, pos_spans, vel_spans))
        on_particles = jnp.transpose(on_particles, (1, 0, 2, 3)).reshape(3, FBLOCKS, slot_count)
        on_faces = jnp.transpose(on_faces, (0, 2, 1, 3)).reshape(FBLOCKS, 3, faces)
        total_push = total_push.at[:, block_t, block_c, :].add(on_particles)
        velocity = velocity + time_step * (total_push + fall)
        offsets = offsets + time_step * velocity
        reaction = reaction + on_faces
    return (offsets, velocity, time_step * reaction)
```

```python
import functools

import jax
import jax.numpy as jnp
from jax import lax
from jax.experimental import pallas as pl
from jax.experimental.pallas import tpu as pltpu
from jax.sharding import PartitionSpec as P

radius = 0.1
face_radius = 0.15
stiffness = 100.0
damping = 40.0
soften = 0.05
time_step = 0.02
gravity = 9.81
away = 1.0e6

F32 = jnp.float32
MESH = pl.DeviceIdType.MESH
VM = pl.BlockSpec(memory_space=pltpu.VMEM)
SM = pl.BlockSpec(memory_space=pltpu.SMEM)
SIDES = [(a, b) for a in (-1, 0, 1) for b in (-1, 0, 1) if (a, b) != (0, 0)]
N_PEERS = 64


def rows():
    return lax.broadcasted_iota(jnp.int32, (8, 128), 0)


def lanes():
    return lax.broadcasted_iota(jnp.int32, (8, 128), 1)


def roll(tile, shift):
    return pltpu.roll(tile, shift, axis=0)


def resting(sign):
    return jnp.where(rows() == 2, sign * away, 0.0)


def scaled(tile):
    row = rows()
    return jnp.where(row < 3, tile, jnp.where(row < 6, -damping * tile, 0.0))


def spread(tile):
    return [jnp.broadcast_to(tile[channel : channel + 1], (8, 128)) for channel in range(6)]


def pushes(own, other, reach):
    x, y, z = (own[axis] - other[axis] for axis in range(3))
    square = x * x + (y * y + (z * z + soften * soften))
    inverse = lax.rsqrt(square)
    depth = jnp.maximum(reach - square * inverse, 0.0) * inverse
    closing = (own[3] - other[3]) * x + (own[4] - other[4]) * y + (own[5] - other[5]) * z
    weight = depth * (stiffness + closing * inverse)
    return weight * x, weight * y, weight * z


def across_lanes(sums_ref, cell):
    found = [jnp.sum(sums_ref[cell, axis].T, axis=0, keepdims=True) for axis in range(3)]
    return jnp.concatenate(found + [jnp.zeros((5, 128), F32)], axis=0)


def place():
    track = lax.axis_index("track")
    cross = lax.axis_index("cross")
    return lax.axis_index("vehicle"), track, cross


def peer_at(step, sign):
    _, track, cross = place()
    dz, dx, dc = step % 8, (step // 8) % 4, step // 32
    x = (track // 4 + 4 + sign * dx) % 4
    z = (cross * 2 + (track // 2) % 2 + 8 + sign * dz) % 8
    core = (track % 2 + dc) % 2
    return x * 4 + (z % 2) * 2 + core, z // 2


def neighbour(side):
    vehicle, track, cross = place()
    row = (vehicle * 16 + track + 64 + side[0]) % 64
    return row // 16, row % 16, (cross + 4 + side[1]) % 4


def greet():
    vehicle = lax.axis_index("vehicle")
    barrier = pltpu.get_barrier_semaphore()

    def one(step, carry):
        track, cross = peer_at(step, 1)
        pl.semaphore_signal(
            barrier, inc=1, device_id=(vehicle, track, cross), device_id_type=MESH
        )
        return carry

    for side in SIDES:
        pl.semaphore_signal(barrier, inc=1, device_id=neighbour(side), device_id_type=MESH)
    lax.fori_loop(1, N_PEERS, one, 0)
    pl.semaphore_wait(barrier, N_PEERS - 1 + len(SIDES))


def halo_copy(index, ring, send_sem, recv_sem):
    down, right = SIDES[index]
    source_row = {1: pl.ds(2, 1), -1: pl.ds(1, 1), 0: pl.ds(1, 2)}[down]
    target_row = {1: pl.ds(0, 1), -1: pl.ds(3, 1), 0: pl.ds(1, 2)}[down]
    source_column = {1: pl.ds(8, 1), -1: pl.ds(1, 1), 0: pl.ds(1, 8)}[right]
    target_column = {1: pl.ds(0, 1), -1: pl.ds(9, 1), 0: pl.ds(1, 8)}[right]
    return pltpu.make_async_remote_copy(
        src_ref=ring.at[source_row, source_column],
        dst_ref=ring.at[target_row, target_column],
        send_sem=send_sem.at[index],
        recv_sem=recv_sem.at[index],
        device_id=neighbour(SIDES[index]),
        device_id_type=MESH,
    )


def block_copy(step, outgoing, incoming, send_sem, recv_sem):
    vehicle, track, cross = place()
    to_track, to_cross = peer_at(step, 1)
    return pltpu.make_async_remote_copy(
        src_ref=outgoing.at[to_track * 4 + to_cross],
        dst_ref=incoming.at[track * 4 + cross],
        send_sem=send_sem.at[step],
        recv_sem=recv_sem.at[step],
        device_id=(vehicle, to_track, to_cross),
        device_id_type=MESH,
    )


def order(turn):
    return (turn * 21) % 64


def set_up_cells(state_ref, count_ref, columns_ref, ring_ref=None):
    def one(cell, carry):
        alive = lanes() < count_ref[cell // 8, cell % 8]
        tile = scaled(state_ref[cell])
        own = jnp.where(alive, tile, resting(1.0))
        for channel in range(6):
            line = jnp.broadcast_to(own[channel : channel + 1], (128, 128))
            columns_ref[cell, channel] = line.T
        if ring_ref is not None:
            ring_ref[cell // 8 + 1, cell % 8 + 1] = jnp.where(alive, tile, resting(-1.0))
        return carry

    lax.fori_loop(0, 16, one, 0)


def clear_edges(ring_ref):
    vehicle, track, cross = place()
    line = vehicle * 16 + track
    dead = resting(-1.0)

    @pl.when(line == 0)
    def _():
        for column in range(10):
            ring_ref[0, column] = dead

    @pl.when(line == 63)
    def _():
        for column in range(10):
            ring_ref[3, column] = dead

    @pl.when(cross == 0)
    def _():
        for row in range(4):
            ring_ref[row, 0] = dead

    @pl.when(cross == 3)
    def _():
        for row in range(4):
            ring_ref[row, 9] = dead


def particle_pushes(ring_ref, columns_ref, sums_ref, out_ref):
    width = 2

    def one(turn, carry):
        cell = turn // (16 // width)
        row_index, column = cell // 8, cell % 8
        for part in range(width):
            start = pl.multiple_of((turn % (16 // width)) * (8 * width) + 8 * part, 8)
            own = [columns_ref[cell, channel, pl.ds(start, 8), :] for channel in range(6)]
            total = [0.0, 0.0, 0.0]
            for down in (-1, 0, 1):
                for right in (-1, 0, 1):
                    other = spread(ring_ref[row_index + 1 + down, column + 1 + right])
                    shifted = [own[0] - float(down), own[1] - float(right)] + own[2:]
                    push = pushes(shifted, other, 2.0 * radius)
                    total = [total[axis] + push[axis] for axis in range(3)]
            for axis in range(3):
                sums_ref[cell, axis, pl.ds(start, 8), :] = total[axis]
        return carry

    lax.fori_loop(0, 256 // width, one, 0)

    def gather(cell, carry):
        out_ref[cell] = across_lanes(sums_ref, cell)
        return carry

    lax.fori_loop(0, 16, gather, 0)


def pack_kernel(po_ref, pv_ref, fo_ref, fv_ref, route_ref, cell_ref, state_ref, send_ref, meta_ref, pos_ref, used):
    for row in range(2):
        for column in range(8):
            cell = row * 8 + column
            for channel in range(3):
                state_ref[cell, channel : channel + 1, :] = po_ref[channel, row, column : column + 1, :]
                state_ref[cell, channel + 3 : channel + 4, :] = pv_ref[channel, row, column : column + 1, :]
            state_ref[cell, 6:8, :] = jnp.zeros((2, 128), F32)
    meta_ref[...] = jnp.full(meta_ref.shape, -1, jnp.int32)

    def clear(index, carry):
        used[index] = 0
        return carry

    lax.fori_loop(0, N_PEERS, clear, 0)
    lane = lax.broadcasted_iota(jnp.int32, (1, 128), 1)

    def one(block, carry):
        target = route_ref[block, 0]
        slot = used[target]
        used[target] = slot + 1
        pos_ref[block] = target * 4 + slot
        meta_ref[target] = jnp.where(lane == slot, cell_ref[block], meta_ref[target])
        for channel in range(3):
            send_ref[target, pl.ds(slot * 6 + channel, 1), :] = fo_ref[block, channel : channel + 1, :]
            send_ref[target, pl.ds(slot * 6 + 3 + channel, 1), :] = fv_ref[block, channel : channel + 1, :]
        return carry

    lax.fori_loop(0, N_PEERS, one, 0)


def first_kernel(
    state_ref, send_ref, meta_ref, count_ref,
    faces_ref, cells_ref, push_ref,
    recv, recv_meta, ring, columns, sums,
    data_out, data_in, meta_out, meta_in, halo_out, halo_in,
):
    _, track, cross = place()
    me = track * 4 + cross
    set_up_cells(state_ref, count_ref, columns, ring)
    greet()
    for index in range(8):
        halo_copy(index, ring, halo_out, halo_in).start()

    def start(turn, carry):
        step = order(turn)
        block_copy(step, meta_ref, recv_meta, meta_out, meta_in).start()
        block_copy(step, send_ref, recv, data_out, data_in).start()
        return carry

    lax.fori_loop(1, N_PEERS, start, 0)
    for index in range(8):
        halo_copy(index, ring, halo_out, halo_in).wait()
    clear_edges(ring)
    particle_pushes(ring, columns, sums, push_ref)
    for slot in range(4):
        faces_ref[me * 4 + slot, 0:6, :] = send_ref[me, slot * 6 : slot * 6 + 6, :]
    cells_ref[me] = meta_ref[me]

    def finish(turn, carry):
        step = order(turn)
        block_copy(step, meta_ref, recv_meta, meta_out, meta_in).wait()
        block_copy(step, send_ref, recv, data_out, data_in).wait()
        from_track, from_cross = peer_at(step, -1)
        source = from_track * 4 + from_cross
        for slot in range(4):
            faces_ref[source * 4 + slot, 0:6, :] = recv[source, slot * 6 : slot * 6 + 6, :]
        cells_ref[source] = recv_meta[source]
        return carry

    lax.fori_loop(1, N_PEERS, finish, 0)


def face_kernel(
    faces_ref, cells_ref, state_ref, push_ref, count_ref,
    next_ref, later_ref, impulse_ref,
    columns, sums, total, reaction, listing,
):
    def gather(index, found):
        listing[found] = index
        return found + (cells_ref[index // 4, 0, index % 4] >= 0).astype(jnp.int32)

    found = lax.fori_loop(0, 256, gather, 0, unroll=8)

    def sweep(second_step):
        sums[...] = jnp.zeros_like(sums)

        def one(turn, carry):
            slot = listing[turn]
            cell = cells_ref[slot // 4, 0, slot % 4]
            tile = faces_ref[slot]
            row = rows()
            tile = jnp.where(row < 6, tile, 0.0)
            if second_step:
                tile = tile + jnp.where(row < 3, time_step * roll(tile, 5), 0.0)
            other = spread(scaled(tile))
            spans = (count_ref[cell // 8, cell % 8] + 31) // 32

            def meet(count):
                back = [0.0, 0.0, 0.0]
                for part in range(count):
                    span = slice(8 * part, 8 * part + 8)
                    own = [columns[cell, channel, span, :] for channel in range(6)]
                    push = pushes(own, other, radius + face_radius)
                    for axis in range(3):
                        sums[cell, axis, span, :] = sums[cell, axis, span, :] + push[axis]
                        back[axis] = back[axis] + push[axis]
                for axis in range(3):
                    line = -time_step * jnp.sum(back[axis], axis=0, keepdims=True)
                    if second_step:
                        impulse_ref[slot, axis : axis + 1, :] = reaction[slot, axis : axis + 1, :] + line
                    else:
                        reaction[slot, axis : axis + 1, :] = line

            for number in range(1, 5):
                pl.when(spans == number)(functools.partial(meet, 4 * number))
            return carry

        lax.fori_loop(0, found, one, 0)

        def collect(cell, carry):
            total[cell] = across_lanes(sums, cell)
            return carry

        lax.fori_loop(0, 16, collect, 0)

    set_up_cells(state_ref, count_ref, columns)
    sweep(False)

    def advance(cell, carry):
        next_ref[cell] = advanced(
            state_ref[cell], push_ref[cell] + total[cell], count_ref[cell // 8, cell % 8]
        )
        return carry

    lax.fori_loop(0, 16, advance, 0)
    set_up_cells(next_ref, count_ref, columns)
    sweep(True)
    later_ref[...] = total[...]


def advanced(tile, push, count):
    row = rows()
    force = jnp.where((row < 3) & (lanes() < count), push, 0.0)
    force = force + jnp.where(row == 2, -gravity, 0.0)
    tile = tile + jnp.where((row >= 3) & (row < 6), time_step * roll(force, 3), 0.0)
    return tile + jnp.where(row < 3, time_step * roll(tile, 5), 0.0)


def second_kernel(
    state_ref, impulse_ref, count_ref,
    push_ref, back_ref,
    outgoing, recv, ring, columns, sums,
    data_out, data_in, halo_out, halo_in,
):
    _, track, cross = place()
    me = track * 4 + cross
    set_up_cells(state_ref, count_ref, columns, ring)
    greet()
    for index in range(8):
        halo_copy(index, ring, halo_out, halo_in).start()

    def start(turn, carry):
        step = order(turn)
        to_track, to_cross = peer_at(step, 1)
        target = to_track * 4 + to_cross
        for slot in range(4):
            outgoing[target, slot * 3 : slot * 3 + 3, :] = impulse_ref[target * 4 + slot, 0:3, :]
        block_copy(step, outgoing, recv, data_out, data_in).start()
        return carry

    lax.fori_loop(1, N_PEERS, start, 0)
    for index in range(8):
        halo_copy(index, ring, halo_out, halo_in).wait()
    clear_edges(ring)
    particle_pushes(ring, columns, sums, push_ref)
    for slot in range(4):
        back_ref[me * 4 + slot] = impulse_ref[me * 4 + slot, 0:3, :]

    def finish(turn, carry):
        step = order(turn)
        block_copy(step, outgoing, recv, data_out, data_in).wait()
        from_track, from_cross = peer_at(step, -1)
        source = from_track * 4 + from_cross
        for slot in range(4):
            back_ref[source * 4 + slot] = recv[source, slot * 3 : slot * 3 + 3, :]
        return carry

    lax.fori_loop(1, N_PEERS, finish, 0)


def last_kernel(state_ref, push_ref, later_ref, count_ref, back_ref, pos_ref, offset_ref, velocity_ref, impulse_ref):
    for row in range(2):
        for column in range(8):
            cell = row * 8 + column
            tile = advanced(state_ref[cell], push_ref[cell] + later_ref[cell], count_ref[row, column])
            for channel in range(3):
                offset_ref[channel, row, column : column + 1, :] = tile[channel : channel + 1]
                velocity_ref[channel, row, column : column + 1, :] = tile[channel + 3 : channel + 4]

    def one(block, carry):
        impulse_ref[block] = back_ref[pos_ref[block]]
        return carry

    lax.fori_loop(0, N_PEERS, one, 0, unroll=4)


def body(particle_offset, particle_velocity, cell_count, face_offset, face_velocity, face_route, face_cell):
    shape = jax.ShapeDtypeStruct
    tiles = shape((16, 8, 128), F32)
    limit = 48 * 1024 * 1024
    plain = pltpu.CompilerParams(vmem_limit_bytes=limit)

    def talking(name):
        return pltpu.CompilerParams(
            vmem_limit_bytes=limit, collective_id=name, has_side_effects=True
        )

    state, send, meta, pos = pl.pallas_call(
        pack_kernel,
        out_shape=(tiles, shape((64, 24, 128), F32), shape((64, 1, 128), jnp.int32), shape((64,), jnp.int32)),
        in_specs=[VM, VM, VM, VM, SM, SM],
        out_specs=(VM, VM, VM, SM),
        scratch_shapes=[pltpu.SMEM((64,), jnp.int32)],
        compiler_params=plain,
        name="pack",
    )(particle_offset, particle_velocity, face_offset, face_velocity, face_route, face_cell)

    cell_scratch = [
        pltpu.VMEM((16, 6, 128, 128), F32),
        pltpu.VMEM((16, 3, 128, 128), F32),
    ]
    sems = [pltpu.SemaphoreType.DMA((64,))] * 2
    halo_sems = [pltpu.SemaphoreType.DMA((8,))] * 2
    faces, cells, push = pl.pallas_call(
        first_kernel,
        out_shape=(shape((256, 8, 128), F32), shape((64, 1, 128), jnp.int32), tiles),
        in_specs=[VM, VM, VM, SM],
        out_specs=(VM, VM, VM),
        scratch_shapes=[
            pltpu.VMEM((64, 24, 128), F32),
            pltpu.VMEM((64, 1, 128), jnp.int32),
            pltpu.VMEM((4, 10, 8, 128), F32),
            *cell_scratch, *sems, *sems, *halo_sems,
        ],
        compiler_params=talking(0),
        name="exchange_faces",
    )(state, send, meta, cell_count)

    state, later, impulse = pl.pallas_call(
        face_kernel,
        out_shape=(tiles, tiles, shape((256, 8, 128), F32)),
        in_specs=[VM, SM, VM, VM, SM],
        out_specs=(VM, VM, VM),
        scratch_shapes=[
            *cell_scratch,
            pltpu.VMEM((16, 8, 128), F32),
            pltpu.VMEM((256, 8, 128), F32),
            pltpu.SMEM((264,), jnp.int32),
        ],
        compiler_params=plain,
        name="faces",
    )(faces, cells, state, push, cell_count)

    push, back = pl.pallas_call(
        second_kernel,
        out_shape=(tiles, shape((256, 3, 128), F32)),
        in_specs=[VM, VM, SM],
        out_specs=(VM, VM),
        scratch_shapes=[
            pltpu.VMEM((64, 12, 128), F32),
            pltpu.VMEM((64, 12, 128), F32),
            pltpu.VMEM((4, 10, 8, 128), F32),
            *cell_scratch, *sems, *halo_sems,
        ],
        compiler_params=talking(1),
        name="exchange_impulses",
    )(state, impulse, cell_count)

    return pl.pallas_call(
        last_kernel,
        out_shape=(
            shape(particle_offset.shape, F32),
            shape(particle_velocity.shape, F32),
            shape(face_offset.shape, F32),
        ),
        in_specs=[VM, VM, VM, SM, VM, SM],
        out_specs=(VM, VM, VM),
        compiler_params=plain,
        name="finish",
    )(state, push, later, cell_count, back, pos)


def solution(mesh):
    everyone = ("vehicle", "track", "cross")
    in_specs = (
        P(None, ("vehicle", "track"), "cross", None),
        P(None, ("vehicle", "track"), "cross", None),
        P(("vehicle", "track"), "cross"),
        P(everyone, None, None),
        P(everyone, None, None),
        P(everyone, None),
        P(everyone),
    )
    out_specs = (
        P(None, ("vehicle", "track"), "cross", None),
        P(None, ("vehicle", "track"), "cross", None),
        P(everyone, None, None),
    )
    return jax.shard_map(body, mesh=mesh, in_specs=in_specs, out_specs=out_specs, check_vma=False)
```

```python
import functools

import jax
import jax.numpy as jnp
from jax import lax
from jax.experimental import pallas as pl
from jax.experimental.pallas import tpu as pltpu
from jax.sharding import PartitionSpec as P

radius = 0.1
face_radius = 0.15
stiffness = 100.0
damping = 40.0
soften = 0.05
time_step = 0.02
gravity = 9.81
away = 1.0e6

F32 = jnp.float32
BF16 = jnp.bfloat16
MESH = pl.DeviceIdType.MESH
VM = pl.BlockSpec(memory_space=pltpu.VMEM)
SM = pl.BlockSpec(memory_space=pltpu.SMEM)
SIDES = [(a, b) for a in (-1, 0, 1) for b in (-1, 0, 1) if (a, b) != (0, 0)]
N_PEERS = 64
WIDTH = 2


def rows():
    return lax.broadcasted_iota(jnp.int32, (8, 128), 0)


def lanes():
    return lax.broadcasted_iota(jnp.int32, (8, 128), 1)


def roll(tile, shift):
    return pltpu.roll(tile, shift, axis=0)


def resting(sign):
    return jnp.where(rows() == 2, sign * away, 0.0)


def scaled(tile):
    row = rows()
    return jnp.where(row < 3, tile, jnp.where(row < 6, -damping * tile, 0.0))


def spread(tile):
    return [jnp.broadcast_to(tile[channel : channel + 1], (8, 128)) for channel in range(6)]


def pushes(own, other, reach):
    x, y, z = (own[axis] - other[axis] for axis in range(3))
    square = x * x + (y * y + (z * z + soften * soften))
    inverse = lax.rsqrt(square)
    depth = jnp.maximum(reach * inverse - 1.0, 0.0)
    closing = (own[3] - other[3]) * x + (own[4] - other[4]) * y + (own[5] - other[5]) * z
    weight = depth * (stiffness + closing * inverse)
    return weight * x, weight * y, weight * z


def across_lanes(sums_ref, cell):
    found = [jnp.sum(sums_ref[cell, axis].T, axis=0, keepdims=True) for axis in range(3)]
    return jnp.concatenate(found + [jnp.zeros((5, 128), F32)], axis=0)


def place():
    track = lax.axis_index("track")
    cross = lax.axis_index("cross")
    return lax.axis_index("vehicle"), track, cross


def peer_at(step, sign):
    _, track, cross = place()
    dz, rest = lax.rem(step, 8), lax.div(step, 8)
    dx, dc = lax.rem(rest, 4), lax.div(rest, 4)
    x = lax.rem(lax.div(track, 4) + 4 + sign * dx, 4)
    z = lax.rem(cross * 2 + lax.rem(lax.div(track, 2), 2) + 8 + sign * dz, 8)
    core = lax.rem(lax.rem(track, 2) + dc, 2)
    return x * 4 + lax.rem(z, 2) * 2 + core, lax.div(z, 2)


def neighbour(side):
    vehicle, track, cross = place()
    row = lax.rem(vehicle * 16 + track + 64 + side[0], 64)
    return lax.div(row, 16), lax.rem(row, 16), lax.rem(cross + 4 + side[1], 4)


def greet():
    vehicle = lax.axis_index("vehicle")
    barrier = pltpu.get_barrier_semaphore()

    def one(step, carry):
        track, cross = peer_at(step, 1)
        pl.semaphore_signal(
            barrier, inc=1, device_id=(vehicle, track, cross), device_id_type=MESH
        )
        return carry

    for side in SIDES:
        pl.semaphore_signal(barrier, inc=1, device_id=neighbour(side), device_id_type=MESH)
    lax.fori_loop(1, N_PEERS, one, 0)


def meet_all():
    pl.semaphore_wait(pltpu.get_barrier_semaphore(), N_PEERS - 1 + len(SIDES))


def halo_copy(index, ring, send_sem, recv_sem):
    down, right = SIDES[index]
    source_row = {1: pl.ds(2, 1), -1: pl.ds(1, 1), 0: pl.ds(1, 2)}[down]
    target_row = {1: pl.ds(0, 1), -1: pl.ds(3, 1), 0: pl.ds(1, 2)}[down]
    source_column = {1: pl.ds(8, 1), -1: pl.ds(1, 1), 0: pl.ds(1, 8)}[right]
    target_column = {1: pl.ds(0, 1), -1: pl.ds(9, 1), 0: pl.ds(1, 8)}[right]
    return pltpu.make_async_remote_copy(
        src_ref=ring.at[source_row, source_column],
        dst_ref=ring.at[target_row, target_column],
        send_sem=send_sem.at[index],
        recv_sem=recv_sem.at[index],
        device_id=neighbour(SIDES[index]),
        device_id_type=MESH,
    )


def block_copy(step, outgoing, incoming, send_sem, recv_sem):
    vehicle, track, cross = place()
    to_track, to_cross = peer_at(step, 1)
    return pltpu.make_async_remote_copy(
        src_ref=outgoing.at[to_track * 4 + to_cross],
        dst_ref=incoming.at[track * 4 + cross],
        send_sem=send_sem.at[step],
        recv_sem=recv_sem.at[step],
        device_id=(vehicle, to_track, to_cross),
        device_id_type=MESH,
    )


def order(turn):
    return lax.rem(turn * 21, 64)


def parts3(tile):
    high = tile.astype(BF16).astype(F32)
    rest = tile - high
    middle = rest.astype(BF16).astype(F32)
    return high, middle, rest - middle


def set_up_cells(state_ref, count_ref, columns_ref, ring_ref=None):
    line = lax.broadcasted_iota(jnp.int32, (32, 768), 0)
    lane = lax.broadcasted_iota(jnp.int32, (32, 768), 1)
    chosen = (lax.rem(line, 8) == lax.div(lane, 128)) & (line < 24)
    pick = jnp.where(chosen, 1.0, 0.0).astype(BF16)
    for cell in range(16):
        alive = lanes() < count_ref[cell // 8, cell % 8]
        tile = scaled(state_ref[cell])
        own = jnp.where(alive, tile, resting(1.0))
        stack = jnp.concatenate([*parts3(own), jnp.zeros((8, 128), F32)], axis=0)
        wide = jnp.dot(stack.T.astype(BF16), pick, preferred_element_type=F32)
        for channel in range(6):
            columns_ref[cell, channel] = wide[:, 128 * channel : 128 * channel + 128]
        if ring_ref is not None:
            ring_ref[cell // 8 + 1, cell % 8 + 1] = jnp.where(alive, tile, resting(-1.0))


def clear_edges(ring_ref):
    vehicle, track, cross = place()
    line = vehicle * 16 + track
    dead = resting(-1.0)

    @pl.when(line == 0)
    def _():
        for column in range(10):
            ring_ref[0, column] = dead

    @pl.when(line == 63)
    def _():
        for column in range(10):
            ring_ref[3, column] = dead

    @pl.when(cross == 0)
    def _():
        for row in range(4):
            ring_ref[row, 0] = dead

    @pl.when(cross == 3)
    def _():
        for row in range(4):
            ring_ref[row, 9] = dead


def particle_pushes(ring_ref, columns_ref, sums_ref, out_ref):
    width = 2

    def one(turn, carry):
        cell = turn // (16 // width)
        row_index, column = cell // 8, cell % 8
        for part in range(width):
            start = pl.multiple_of((turn % (16 // width)) * (8 * width) + 8 * part, 8)
            own = [columns_ref[cell, channel, pl.ds(start, 8), :] for channel in range(6)]
            total = [0.0, 0.0, 0.0]
            for down in (-1, 0, 1):
                for right in (-1, 0, 1):
                    other = spread(ring_ref[row_index + 1 + down, column + 1 + right])
                    shifted = [own[0] - float(down), own[1] - float(right)] + own[2:]
                    push = pushes(shifted, other, 2.0 * radius)
                    total = [total[axis] + push[axis] for axis in range(3)]
            for axis in range(3):
                sums_ref[cell, axis, pl.ds(start, 8), :] = total[axis]
        return carry

    lax.fori_loop(0, 256 // width, one, 0)

    def gather(cell, carry):
        out_ref[cell] = across_lanes(sums_ref, cell)
        return carry

    lax.fori_loop(0, 16, gather, 0, unroll=4)


def pack_kernel(po_ref, pv_ref, fo_ref, fv_ref, route_ref, cell_ref, state_ref, send_ref, meta_ref, pos_ref, used):
    for row in range(2):
        for column in range(8):
            cell = row * 8 + column
            for channel in range(3):
                state_ref[cell, channel : channel + 1, :] = po_ref[channel, row, column : column + 1, :]
                state_ref[cell, channel + 3 : channel + 4, :] = pv_ref[channel, row, column : column + 1, :]
            state_ref[cell, 6:8, :] = jnp.zeros((2, 128), F32)
    meta_ref[...] = jnp.full(meta_ref.shape, -1, jnp.int32)

    def clear(index, carry):
        used[index] = 0
        return carry

    lax.fori_loop(0, N_PEERS, clear, 0)
    lane = lax.broadcasted_iota(jnp.int32, (1, 128), 1)

    def one(block, carry):
        target = route_ref[block, 0]
        slot = used[target]
        used[target] = slot + 1
        pos_ref[block] = target * 4 + slot
        meta_ref[target] = jnp.where(lane == slot, cell_ref[block], meta_ref[target])
        for channel in range(3):
            send_ref[target, pl.ds(slot * 6 + channel, 1), :] = fo_ref[block, channel : channel + 1, :]
            send_ref[target, pl.ds(slot * 6 + 3 + channel, 1), :] = fv_ref[block, channel : channel + 1, :]
        return carry

    lax.fori_loop(0, N_PEERS, one, 0)


def first_kernel(
    state_ref, send_ref, meta_ref, count_ref,
    faces_ref, cells_ref, push_ref,
    recv, recv_meta, ring, columns, sums,
    data_out, data_in, meta_out, meta_in, halo_out, halo_in,
):
    _, track, cross = place()
    me = track * 4 + cross
    greet()
    set_up_cells(state_ref, count_ref, columns, ring)
    meet_all()
    for index in range(8):
        halo_copy(index, ring, halo_out, halo_in).start()

    def start(turn, carry):
        step = order(turn)
        block_copy(step, meta_ref, recv_meta, meta_out, meta_in).start()
        block_copy(step, send_ref, recv, data_out, data_in).start()
        return carry

    lax.fori_loop(1, N_PEERS, start, 0)
    for index in range(8):
        halo_copy(index, ring, halo_out, halo_in).wait()
    clear_edges(ring)
    particle_pushes(ring, columns, sums, push_ref)
    for slot in range(4):
        faces_ref[me * 4 + slot, 0:6, :] = send_ref[me, slot * 6 : slot * 6 + 6, :]
    faces_ref[256] = resting(-1.0)
    cells_ref[me] = meta_ref[me]

    def finish(turn, carry):
        step = order(turn)
        block_copy(step, meta_ref, recv_meta, meta_out, meta_in).wait()
        block_copy(step, send_ref, recv, data_out, data_in).wait()
        from_track, from_cross = peer_at(step, -1)
        source = from_track * 4 + from_cross
        for slot in range(4):
            faces_ref[source * 4 + slot, 0:6, :] = recv[source, slot * 6 : slot * 6 + 6, :]
        cells_ref[source] = recv_meta[source]
        return carry

    lax.fori_loop(1, N_PEERS, finish, 0)


def face_kernel(
    faces_ref, cells_ref, state_ref, push_ref, count_ref,
    next_ref, later_ref, impulse_ref,
    columns, sums, now, filled, listing,
):
    room = 256 + WIDTH
    for cell in range(17):
        filled[cell] = 0

    def enter(index, carry):
        named = cells_ref[lax.div(index, 4), 0, lax.rem(index, 4)]
        cell = jnp.where(named >= 0, named, 16)
        count = filled[cell]
        listing[cell * room + count] = index
        filled[cell] = count + 1
        return carry

    lax.fori_loop(0, 256, enter, 0, unroll=4)
    for cell in range(16):
        for extra in range(WIDTH - 1):
            listing[cell * room + filled[cell] + extra] = 256
    now[...] = state_ref[...]

    def substep(step, carry):
        moved = time_step * step.astype(F32)
        sums[...] = jnp.zeros_like(sums)
        set_up_cells(now, count_ref, columns)

        def contacts(cell, count):
            def one(turn, carry):
                slots = [listing[cell * room + turn * WIDTH + index] for index in range(WIDTH)]
                row = rows()
                others = []
                for slot in slots:
                    tile = faces_ref[slot]
                    tile = tile + jnp.where(row < 3, moved * roll(tile, 5), 0.0)
                    others.append(spread(scaled(tile)))
                back = [[0.0, 0.0, 0.0] for _ in slots]
                for part in range(count):
                    span = slice(8 * part, 8 * part + 8)
                    own = [columns[cell, channel, span, :] for channel in range(6)]
                    push = [pushes(own, other, radius + face_radius) for other in others]
                    for axis in range(3):
                        gained = push[0][axis]
                        for other in push[1:]:
                            gained = gained + other[axis]
                        sums[cell, axis, span, :] = sums[cell, axis, span, :] + gained
                        for side in range(WIDTH):
                            back[side][axis] = back[side][axis] + push[side][axis]
                for side in range(WIDTH):
                    lines = [-time_step * jnp.sum(back[side][axis], axis=0, keepdims=True) for axis in range(3)]
                    tile = jnp.concatenate(lines + [jnp.zeros((5, 128), F32)], axis=0)
                    earlier = jnp.where(step == 0, 0.0, impulse_ref[slots[side]])
                    impulse_ref[slots[side]] = earlier + tile
                return carry

            lax.fori_loop(0, lax.div(filled[cell] + WIDTH - 1, WIDTH), one, 0)

        def block(cell, carry):
            spans = lax.div(count_ref[lax.div(cell, 8), lax.rem(cell, 8)] + 15, 16)
            for number in range(2, 9):
                pl.when(spans == number)(functools.partial(contacts, cell, 2 * number))
            return carry

        lax.fori_loop(0, 16, block, 0)

        def collect(cell, carry):
            later_ref[cell] = across_lanes(sums, cell)
            return carry

        lax.fori_loop(0, 16, collect, 0, unroll=4)

        @pl.when(step == 0)
        def _():
            def advance(cell, carry):
                count = count_ref[lax.div(cell, 8), lax.rem(cell, 8)]
                tile = advanced(now[cell], push_ref[cell] + later_ref[cell], count)
                now[cell] = tile
                next_ref[cell] = tile
                return carry

            lax.fori_loop(0, 16, advance, 0, unroll=4)

        return carry

    lax.fori_loop(0, 2, substep, 0)


def advanced(tile, push, count):
    row = rows()
    force = jnp.where((row < 3) & (lanes() < count), push, 0.0)
    force = force + jnp.where(row == 2, -gravity, 0.0)
    tile = tile + jnp.where((row >= 3) & (row < 6), time_step * roll(force, 3), 0.0)
    return tile + jnp.where(row < 3, time_step * roll(tile, 5), 0.0)


def second_kernel(
    state_ref, impulse_ref, count_ref,
    push_ref, back_ref,
    outgoing, recv, ring, columns, sums,
    data_out, data_in, halo_out, halo_in,
):
    _, track, cross = place()
    me = track * 4 + cross
    greet()
    set_up_cells(state_ref, count_ref, columns, ring)
    meet_all()
    for index in range(8):
        halo_copy(index, ring, halo_out, halo_in).start()

    def start(turn, carry):
        step = order(turn)
        to_track, to_cross = peer_at(step, 1)
        target = to_track * 4 + to_cross
        for slot in range(4):
            outgoing[target, slot * 3 : slot * 3 + 3, :] = impulse_ref[target * 4 + slot, 0:3, :]
        block_copy(step, outgoing, recv, data_out, data_in).start()
        return carry

    lax.fori_loop(1, N_PEERS, start, 0)
    for index in range(8):
        halo_copy(index, ring, halo_out, halo_in).wait()
    clear_edges(ring)
    particle_pushes(ring, columns, sums, push_ref)
    for slot in range(4):
        back_ref[me * 4 + slot] = impulse_ref[me * 4 + slot, 0:3, :]

    def finish(turn, carry):
        step = order(turn)
        block_copy(step, outgoing, recv, data_out, data_in).wait()
        from_track, from_cross = peer_at(step, -1)
        source = from_track * 4 + from_cross
        for slot in range(4):
            back_ref[source * 4 + slot] = recv[source, slot * 3 : slot * 3 + 3, :]
        return carry

    lax.fori_loop(1, N_PEERS, finish, 0)


def last_kernel(state_ref, push_ref, later_ref, count_ref, back_ref, pos_ref, offset_ref, velocity_ref, impulse_ref):
    for row in range(2):
        for column in range(8):
            cell = row * 8 + column
            tile = advanced(state_ref[cell], push_ref[cell] + later_ref[cell], count_ref[row, column])
            for channel in range(3):
                offset_ref[channel, row, column : column + 1, :] = tile[channel : channel + 1]
                velocity_ref[channel, row, column : column + 1, :] = tile[channel + 3 : channel + 4]

    def one(block, carry):
        impulse_ref[block] = back_ref[pos_ref[block]]
        return carry

    lax.fori_loop(0, N_PEERS, one, 0, unroll=4)


def body(particle_offset, particle_velocity, cell_count, face_offset, face_velocity, face_route, face_cell):
    shape = jax.ShapeDtypeStruct
    tiles = shape((16, 8, 128), F32)
    limit = 48 * 1024 * 1024
    plain = pltpu.CompilerParams(vmem_limit_bytes=limit)

    def talking(name):
        return pltpu.CompilerParams(
            vmem_limit_bytes=limit, collective_id=name, has_side_effects=True
        )

    state, send, meta, pos = pl.pallas_call(
        pack_kernel,
        out_shape=(tiles, shape((64, 24, 128), F32), shape((64, 1, 128), jnp.int32), shape((64,), jnp.int32)),
        in_specs=[VM, VM, VM, VM, SM, SM],
        out_specs=(VM, VM, VM, SM),
        scratch_shapes=[pltpu.SMEM((64,), jnp.int32)],
        compiler_params=plain,
        name="pack",
    )(particle_offset, particle_velocity, face_offset, face_velocity, face_route, face_cell)

    cell_scratch = [
        pltpu.VMEM((16, 6, 128, 128), F32),
        pltpu.VMEM((16, 3, 128, 128), F32),
    ]
    sems = [pltpu.SemaphoreType.DMA((64,))] * 2
    halo_sems = [pltpu.SemaphoreType.DMA((8,))] * 2
    faces, cells, push = pl.pallas_call(
        first_kernel,
        out_shape=(shape((257, 8, 128), F32), shape((64, 1, 128), jnp.int32), tiles),
        in_specs=[VM, VM, VM, SM],
        out_specs=(VM, VM, VM),
        scratch_shapes=[
            pltpu.VMEM((64, 24, 128), F32),
            pltpu.VMEM((64, 1, 128), jnp.int32),
            pltpu.VMEM((4, 10, 8, 128), F32),
            *cell_scratch, *sems, *sems, *halo_sems,
        ],
        compiler_params=talking(0),
        name="exchange_faces",
    )(state, send, meta, cell_count)

    state, later, impulse = pl.pallas_call(
        face_kernel,
        out_shape=(tiles, tiles, shape((257, 8, 128), F32)),
        in_specs=[VM, SM, VM, VM, SM],
        out_specs=(VM, VM, VM),
        scratch_shapes=[
            *cell_scratch,
            pltpu.VMEM((16, 8, 128), F32),
            pltpu.SMEM((17,), jnp.int32),
            pltpu.SMEM((17 * (256 + WIDTH),), jnp.int32),
        ],
        compiler_params=plain,
        name="faces",
    )(faces, cells, state, push, cell_count)

    push, back = pl.pallas_call(
        second_kernel,
        out_shape=(tiles, shape((256, 3, 128), F32)),
        in_specs=[VM, VM, SM],
        out_specs=(VM, VM),
        scratch_shapes=[
            pltpu.VMEM((64, 12, 128), F32),
            pltpu.VMEM((64, 12, 128), F32),
            pltpu.VMEM((4, 10, 8, 128), F32),
            *cell_scratch, *sems, *halo_sems,
        ],
        compiler_params=talking(1),
        name="exchange_impulses",
    )(state, impulse, cell_count)

    return pl.pallas_call(
        last_kernel,
        out_shape=(
            shape(particle_offset.shape, F32),
            shape(particle_velocity.shape, F32),
            shape(face_offset.shape, F32),
        ),
        in_specs=[VM, VM, VM, SM, VM, SM],
        out_specs=(VM, VM, VM),
        compiler_params=plain,
        name="finish",
    )(state, push, later, cell_count, back, pos)


def solution(mesh):
    everyone = ("vehicle", "track", "cross")
    in_specs = (
        P(None, ("vehicle", "track"), "cross", None),
        P(None, ("vehicle", "track"), "cross", None),
        P(("vehicle", "track"), "cross"),
        P(everyone, None, None),
        P(everyone, None, None),
        P(everyone, None),
        P(everyone),
    )
    out_specs = (
        P(None, ("vehicle", "track"), "cross", None),
        P(None, ("vehicle", "track"), "cross", None),
        P(everyone, None, None),
    )
    return jax.shard_map(body, mesh=mesh, in_specs=in_specs, out_specs=out_specs, check_vma=False)
```

```python
import functools

import jax
import jax.numpy as jnp
from jax import lax
from jax.experimental import pallas as pl
from jax.experimental.pallas import tpu as pltpu
from jax.sharding import PartitionSpec as P

radius = 0.1
face_radius = 0.15
stiffness = 100.0
damping = 40.0
soften = 0.05
time_step = 0.02
gravity = 9.81
away = 1.0e6

F32 = jnp.float32
BF16 = jnp.bfloat16
MESH = pl.DeviceIdType.MESH
VM = pl.BlockSpec(memory_space=pltpu.VMEM)
SM = pl.BlockSpec(memory_space=pltpu.SMEM)
SIDES = [(a, b) for a in (-1, 0, 1) for b in (-1, 0, 1) if (a, b) != (0, 0)]
N_PEERS = 64
COUNTS = 128
PART = 2
WIDTH = 2


def rows():
    return lax.broadcasted_iota(jnp.int32, (8, 128), 0)


def lanes():
    return lax.broadcasted_iota(jnp.int32, (8, 128), 1)


def roll(tile, shift):
    return pltpu.roll(tile, shift, axis=0)


def resting(sign):
    return jnp.where(rows() == 2, sign * away, 0.0)


def scaled(tile, reach):
    row = rows()
    return jnp.where(row < 3, tile, jnp.where(row < 6, (-damping * reach) * tile, 0.0))


def spread(tile):
    return [jnp.broadcast_to(tile[channel : channel + 1], (8, 128)) for channel in range(6)]


def pushes(own, other, reach):
    x, y, z = (own[axis] - other[axis] for axis in range(3))
    square = x * x + (y * y + (z * z + soften * soften))
    inverse = lax.rsqrt(square)
    depth = jnp.maximum(inverse - 1.0 / reach, 0.0)
    closing = (own[3] - other[3]) * x + (own[4] - other[4]) * y + (own[5] - other[5]) * z
    weight = depth * (stiffness * reach + closing * inverse)
    return weight * x, weight * y, weight * z


def across_lanes(sums_ref, cell):
    found = [jnp.sum(sums_ref[cell, axis].T, axis=0, keepdims=True) for axis in range(3)]
    return jnp.concatenate(found + [jnp.zeros((5, 128), F32)], axis=0)


def place():
    track = lax.axis_index("track")
    cross = lax.axis_index("cross")
    return lax.axis_index("vehicle"), track, cross


def peer_at(step, sign):
    _, track, cross = place()
    dz, rest = lax.rem(step, 8), lax.div(step, 8)
    dx, dc = lax.rem(rest, 4), lax.div(rest, 4)
    x = lax.rem(lax.div(track, 4) + 4 + sign * dx, 4)
    z = lax.rem(cross * 2 + lax.rem(lax.div(track, 2), 2) + 8 + sign * dz, 8)
    core = lax.rem(lax.rem(track, 2) + dc, 2)
    return x * 4 + lax.rem(z, 2) * 2 + core, lax.div(z, 2)


def neighbour(side):
    vehicle, track, cross = place()
    row = lax.rem(vehicle * 16 + track + 64 + side[0], 64)
    return lax.div(row, 16), lax.rem(row, 16), lax.rem(cross + 4 + side[1], 4)


def greet():
    vehicle = lax.axis_index("vehicle")
    barrier = pltpu.get_barrier_semaphore()

    def one(step, carry):
        track, cross = peer_at(step, 1)
        pl.semaphore_signal(
            barrier, inc=1, device_id=(vehicle, track, cross), device_id_type=MESH
        )
        return carry

    for side in SIDES:
        pl.semaphore_signal(barrier, inc=1, device_id=neighbour(side), device_id_type=MESH)
    lax.fori_loop(1, N_PEERS, one, 0)


def meet_all():
    pl.semaphore_wait(pltpu.get_barrier_semaphore(), N_PEERS - 1 + len(SIDES))


def halo_copy(index, ring, send_sem, recv_sem):
    down, right = SIDES[index]
    source_row = {1: pl.ds(2, 1), -1: pl.ds(1, 1), 0: pl.ds(1, 2)}[down]
    target_row = {1: pl.ds(0, 1), -1: pl.ds(3, 1), 0: pl.ds(1, 2)}[down]
    source_column = {1: pl.ds(8, 1), -1: pl.ds(1, 1), 0: pl.ds(1, 8)}[right]
    target_column = {1: pl.ds(0, 1), -1: pl.ds(9, 1), 0: pl.ds(1, 8)}[right]
    return pltpu.make_async_remote_copy(
        src_ref=ring.at[source_row, source_column],
        dst_ref=ring.at[target_row, target_column],
        send_sem=send_sem.at[index],
        recv_sem=recv_sem.at[index],
        device_id=neighbour(SIDES[index]),
        device_id_type=MESH,
    )


def block_copy(step, outgoing, incoming, send_sem, recv_sem):
    vehicle, track, cross = place()
    to_track, to_cross = peer_at(step, 1)
    return pltpu.make_async_remote_copy(
        src_ref=outgoing.at[to_track * 4 + to_cross],
        dst_ref=incoming.at[track * 4 + cross],
        send_sem=send_sem.at[step],
        recv_sem=recv_sem.at[step],
        device_id=(vehicle, to_track, to_cross),
        device_id_type=MESH,
    )


def order(turn):
    return lax.rem(turn * 21, 64)


def parts3(tile):
    high = tile.astype(BF16).astype(F32)
    rest = tile - high
    middle = rest.astype(BF16).astype(F32)
    return high, middle, rest - middle


def set_up_cells(state_ref, count_ref, reach, columns_ref, ring_ref=None):
    line = lax.broadcasted_iota(jnp.int32, (32, 768), 0)
    lane = lax.broadcasted_iota(jnp.int32, (32, 768), 1)
    chosen = (lax.rem(line, 8) == lax.div(lane, 128)) & (line < 24)
    pick = jnp.where(chosen, 1.0, 0.0).astype(BF16)
    for cell in range(16):
        alive = lanes() < count_ref[COUNTS + cell]
        tile = scaled(state_ref[cell], reach)
        own = jnp.where(alive, tile, resting(1.0))
        stack = jnp.concatenate([*parts3(own), jnp.zeros((8, 128), F32)], axis=0)
        wide = jnp.dot(stack.T.astype(BF16), pick, preferred_element_type=F32)
        for channel in range(6):
            columns_ref[cell, channel] = wide[:, 128 * channel : 128 * channel + 128]
        if ring_ref is not None:
            ring_ref[cell // 8 + 1, cell % 8 + 1] = jnp.where(alive, tile, resting(-1.0))


def clear_edges(ring_ref):
    vehicle, track, cross = place()
    line = vehicle * 16 + track
    dead = resting(-1.0)

    @pl.when(line == 0)
    def _():
        for column in range(10):
            ring_ref[0, column] = dead

    @pl.when(line == 63)
    def _():
        for column in range(10):
            ring_ref[3, column] = dead

    @pl.when(cross == 0)
    def _():
        for row in range(4):
            ring_ref[row, 0] = dead

    @pl.when(cross == 3)
    def _():
        for row in range(4):
            ring_ref[row, 9] = dead


def meet_blocks(cell, part, blocks, columns_ref, ring_ref, sums_ref, base_ref):
    for piece in range(PART):
        start = pl.multiple_of(part * (8 * PART) + 8 * piece, 8)
        own = [columns_ref[cell, channel, pl.ds(start, 8), :] for channel in range(6)]
        total = [0.0, 0.0, 0.0]
        for row, column, down, right in blocks:
            other = spread(ring_ref[row, column])
            shifted = [own[0] - down, own[1] - right] + own[2:]
            push = pushes(shifted, other, 2.0 * radius)
            total = [total[axis] + push[axis] for axis in range(3)]
        for axis in range(3):
            if base_ref is not None:
                total[axis] = total[axis] + base_ref[cell, axis, pl.ds(start, 8), :]
            sums_ref[cell, axis, pl.ds(start, 8), :] = total[axis]


def inner_pushes(ring_ref, columns_ref, sums_ref, base_ref=None):
    parts = 16 // PART

    def one(turn, carry):
        which, part = lax.div(turn, parts), lax.rem(turn, parts)
        row, column = lax.div(which, 6), lax.rem(which, 6) + 1
        blocks = [
            (other + 1, column + 1 + right, (other - row).astype(F32), float(right))
            for other in range(2)
            for right in (-1, 0, 1)
        ]
        meet_blocks(row * 8 + column, part, blocks, columns_ref, ring_ref, sums_ref, base_ref)
        return carry

    lax.fori_loop(0, 12 * parts, one, 0)


def outer_pushes(ring_ref, columns_ref, sums_ref, out_ref, base_ref=None):
    parts = 16 // PART

    def one(turn, carry):
        which, part = lax.div(turn, parts), lax.rem(turn, parts)
        row, column = lax.div(which, 6), lax.rem(which, 6) + 1
        down = (2 * row - 1).astype(F32)
        blocks = [(3 * row, column + 1 + right, down, float(right)) for right in (-1, 0, 1)]
        meet_blocks(row * 8 + column, part, blocks, columns_ref, ring_ref, sums_ref, sums_ref)
        return carry

    lax.fori_loop(0, 12 * parts, one, 0)

    def side(turn, carry):
        which, part = lax.div(turn, parts), lax.rem(turn, parts)
        row, column = lax.div(which, 2), lax.rem(which, 2) * 7
        blocks = [
            (row + 1 + down, column + 1 + right, float(down), float(right))
            for down in (-1, 0, 1)
            for right in (-1, 0, 1)
        ]
        meet_blocks(row * 8 + column, part, blocks, columns_ref, ring_ref, sums_ref, base_ref)
        return carry

    lax.fori_loop(0, 4 * parts, side, 0)

    def gather(cell, carry):
        out_ref[cell] = across_lanes(sums_ref, cell)
        return carry

    lax.fori_loop(0, 16, gather, 0, unroll=4)


def pack_kernel(parts_ref, blocks_ref, ints_ref, state_ref, send_ref, pos_ref, used):
    send_ref[:, 24:25, :] = jnp.full((N_PEERS, 1, 128), -1.0, F32)

    def clear(index, carry):
        used[index] = 0
        return carry

    lax.fori_loop(0, N_PEERS, clear, 0, unroll=8)
    for row in range(2):
        for column in range(8):
            cell = row * 8 + column
            for channel in range(6):
                state_ref[cell, channel : channel + 1, :] = parts_ref[channel, row, column : column + 1, :]
            state_ref[cell, 6:8, :] = jnp.zeros((2, 128), F32)
    lane = lax.broadcasted_iota(jnp.int32, (1, 128), 1)

    def one(block, carry):
        target = ints_ref[block]
        slot = used[target]
        used[target] = slot + 1
        pos_ref[block] = target * 4 + slot
        touched = ints_ref[N_PEERS + block].astype(F32)
        send_ref[target, 24:25, :] = jnp.where(lane == slot, touched, send_ref[target, 24:25, :])
        for channel in range(6):
            send_ref[target, pl.ds(slot * 6 + channel, 1), :] = blocks_ref[channel, pl.ds(block, 1), :]
        return carry

    lax.fori_loop(0, N_PEERS, one, 0, unroll=4)


def first_kernel(
    state_ref, send_ref, count_ref,
    faces_ref, cells_ref, push_ref,
    recv, ring, columns, sums,
    data_out, data_in, halo_out, halo_in,
):
    _, track, cross = place()
    me = track * 4 + cross
    greet()
    set_up_cells(state_ref, count_ref, 2.0 * radius, columns, ring)
    meet_all()
    for index in range(8):
        halo_copy(index, ring, halo_out, halo_in).start()

    def start(turn, carry):
        step = order(turn)
        block_copy(step, send_ref, recv, data_out, data_in).start()
        return carry

    lax.fori_loop(1, N_PEERS, start, 0)
    inner_pushes(ring, columns, sums)
    for index in range(8):
        halo_copy(index, ring, halo_out, halo_in).wait()
    clear_edges(ring)
    outer_pushes(ring, columns, sums, push_ref)
    for slot in range(4):
        faces_ref[me * 4 + slot, 0:6, :] = send_ref[me, slot * 6 : slot * 6 + 6, :]
    faces_ref[256] = resting(-1.0)
    cells_ref[me] = send_ref[me, 24:25, :]

    def finish(turn, carry):
        step = order(turn)
        block_copy(step, send_ref, recv, data_out, data_in).wait()
        from_track, from_cross = peer_at(step, -1)
        source = from_track * 4 + from_cross
        for slot in range(4):
            faces_ref[source * 4 + slot, 0:6, :] = recv[source, slot * 6 : slot * 6 + 6, :]
        cells_ref[source] = recv[source, 24:25, :]
        return carry

    lax.fori_loop(1, N_PEERS, finish, 0)


def face_kernel(
    faces_ref, cells_ref, state_ref, push_ref, count_ref,
    next_ref, sums, impulse_ref,
    columns, now, filled, listing,
):
    room = 256 + WIDTH
    for cell in range(17):
        filled[cell] = 0

    def enter(index, carry):
        named = cells_ref[lax.div(index, 4), 0, lax.rem(index, 4)].astype(jnp.int32)
        cell = jnp.where(named >= 0, named, 16)
        count = filled[cell]
        listing[cell * room + count] = index
        filled[cell] = count + 1
        return carry

    lax.fori_loop(0, 256, enter, 0, unroll=4)
    for cell in range(16):
        for extra in range(WIDTH - 1):
            listing[cell * room + filled[cell] + extra] = 256
    now[...] = state_ref[...]

    def substep(step, carry):
        moved = time_step * step.astype(F32)
        sums[...] = jnp.zeros_like(sums)
        set_up_cells(now, count_ref, radius + face_radius, columns)

        def contacts(cell, count):
            def one(turn, carry):
                slots = [listing[cell * room + turn * WIDTH + index] for index in range(WIDTH)]
                row = rows()
                others = []
                for slot in slots:
                    tile = faces_ref[slot]
                    tile = tile + jnp.where(row < 3, moved * roll(tile, 5), 0.0)
                    others.append(spread(scaled(tile, radius + face_radius)))
                back = [[0.0, 0.0, 0.0] for _ in slots]
                for part in range(count):
                    span = slice(8 * part, 8 * part + 8)
                    own = [columns[cell, channel, span, :] for channel in range(6)]
                    push = [pushes(own, other, radius + face_radius) for other in others]
                    for axis in range(3):
                        gained = push[0][axis]
                        for other in push[1:]:
                            gained = gained + other[axis]
                        sums[cell, axis, span, :] = sums[cell, axis, span, :] + gained
                        for side in range(WIDTH):
                            back[side][axis] = back[side][axis] + push[side][axis]
                for side in range(WIDTH):
                    lines = [-time_step * jnp.sum(back[side][axis], axis=0, keepdims=True) for axis in range(3)]
                    tile = jnp.concatenate(lines + [jnp.zeros((5, 128), F32)], axis=0)
                    earlier = jnp.where(step == 0, 0.0, impulse_ref[slots[side]])
                    impulse_ref[slots[side]] = earlier + tile
                return carry

            lax.fori_loop(0, lax.div(filled[cell] + WIDTH - 1, WIDTH), one, 0)

        def block(cell, carry):
            spans = lax.div(count_ref[COUNTS + cell] + 7, 8)
            for number in range(4, 17):
                pl.when(spans == number)(functools.partial(contacts, cell, number))
            return carry

        lax.fori_loop(0, 16, block, 0)

        @pl.when(step == 0)
        def _():
            def advance(cell, carry):
                total = push_ref[cell] + across_lanes(sums, cell)
                tile = advanced(now[cell], total, count_ref[COUNTS + cell])
                now[cell] = tile
                next_ref[cell] = tile
                return carry

            lax.fori_loop(0, 16, advance, 0, unroll=4)

        return carry

    lax.fori_loop(0, 2, substep, 0)


def advanced(tile, push, count):
    row = rows()
    force = jnp.where((row < 3) & (lanes() < count), push, 0.0)
    force = force + jnp.where(row == 2, -gravity, 0.0)
    tile = tile + jnp.where((row >= 3) & (row < 6), time_step * roll(force, 3), 0.0)
    return tile + jnp.where(row < 3, time_step * roll(tile, 5), 0.0)


def second_kernel(
    state_ref, impulse_ref, base_ref, count_ref,
    push_ref, back_ref,
    outgoing, recv, ring, columns, sums,
    data_out, data_in, halo_out, halo_in,
):
    _, track, cross = place()
    me = track * 4 + cross
    greet()
    set_up_cells(state_ref, count_ref, 2.0 * radius, columns, ring)
    meet_all()
    for index in range(8):
        halo_copy(index, ring, halo_out, halo_in).start()

    def start(turn, carry):
        step = order(turn)
        to_track, to_cross = peer_at(step, 1)
        target = to_track * 4 + to_cross
        for slot in range(4):
            outgoing[target, slot * 3 : slot * 3 + 3, :] = impulse_ref[target * 4 + slot, 0:3, :]
        block_copy(step, outgoing, recv, data_out, data_in).start()
        return carry

    lax.fori_loop(1, N_PEERS, start, 0)
    inner_pushes(ring, columns, sums, base_ref)
    for index in range(8):
        halo_copy(index, ring, halo_out, halo_in).wait()
    clear_edges(ring)
    outer_pushes(ring, columns, sums, push_ref, base_ref)
    for slot in range(4):
        back_ref[me * 4 + slot] = impulse_ref[me * 4 + slot, 0:3, :]

    def finish(turn, carry):
        step = order(turn)
        block_copy(step, outgoing, recv, data_out, data_in).wait()
        from_track, from_cross = peer_at(step, -1)
        source = from_track * 4 + from_cross
        for slot in range(4):
            back_ref[source * 4 + slot] = recv[source, slot * 3 : slot * 3 + 3, :]
        return carry

    lax.fori_loop(1, N_PEERS, finish, 0)


def last_kernel(state_ref, push_ref, count_ref, back_ref, pos_ref, offset_ref, velocity_ref, impulse_ref):
    for row in range(2):
        for column in range(8):
            cell = row * 8 + column
            tile = advanced(state_ref[cell], push_ref[cell], count_ref[COUNTS + cell])
            for channel in range(3):
                offset_ref[channel, row, column : column + 1, :] = tile[channel : channel + 1]
                velocity_ref[channel, row, column : column + 1, :] = tile[channel + 3 : channel + 4]

    def one(block, carry):
        slot = pos_ref[block]
        for axis in range(3):
            impulse_ref[axis, pl.ds(block, 1), :] = back_ref[slot, axis : axis + 1, :]
        return carry

    lax.fori_loop(0, N_PEERS, one, 0, unroll=4)


def body(particle_offset, particle_velocity, cell_count, face_offset, face_velocity, face_route, face_cell):
    shape = jax.ShapeDtypeStruct
    tiles = shape((16, 8, 128), F32)
    limit = 48 * 1024 * 1024
    plain = pltpu.CompilerParams(vmem_limit_bytes=limit)

    def talking(name):
        return pltpu.CompilerParams(
            vmem_limit_bytes=limit, collective_id=name, has_side_effects=True
        )

    parts = jnp.concatenate([particle_offset, particle_velocity], axis=0)
    blocks = jnp.concatenate(
        [jnp.transpose(face_offset, (1, 0, 2)), jnp.transpose(face_velocity, (1, 0, 2))], axis=0
    )
    ints = jnp.concatenate([face_route.reshape(-1), face_cell, cell_count.reshape(-1)])
    state, send, pos = pl.pallas_call(
        pack_kernel,
        out_shape=(tiles, shape((64, 25, 128), F32), shape((64,), jnp.int32)),
        in_specs=[VM, VM, SM],
        out_specs=(VM, VM, SM),
        scratch_shapes=[pltpu.SMEM((64,), jnp.int32)],
        compiler_params=plain,
        name="pack",
    )(parts, blocks, ints)

    cell_scratch = [
        pltpu.VMEM((16, 6, 128, 128), F32),
        pltpu.VMEM((16, 3, 128, 128), F32),
    ]
    sems = [pltpu.SemaphoreType.DMA((64,))] * 2
    halo_sems = [pltpu.SemaphoreType.DMA((8,))] * 2
    faces, cells, push = pl.pallas_call(
        first_kernel,
        out_shape=(shape((257, 8, 128), F32), shape((64, 1, 128), F32), tiles),
        in_specs=[VM, VM, SM],
        out_specs=(VM, VM, VM),
        scratch_shapes=[
            pltpu.VMEM((64, 25, 128), F32),
            pltpu.VMEM((4, 10, 8, 128), F32),
            *cell_scratch, *sems, *halo_sems,
        ],
        compiler_params=talking(0),
        name="exchange_faces",
    )(state, send, ints)

    state, sums, impulse = pl.pallas_call(
        face_kernel,
        out_shape=(tiles, shape((16, 3, 128, 128), F32), shape((257, 8, 128), F32)),
        in_specs=[VM, SM, VM, VM, SM],
        out_specs=(VM, VM, VM),
        scratch_shapes=[
            cell_scratch[0],
            pltpu.VMEM((16, 8, 128), F32),
            pltpu.SMEM((17,), jnp.int32),
            pltpu.SMEM((17 * (256 + WIDTH),), jnp.int32),
        ],
        compiler_params=plain,
        name="faces",
    )(faces, cells, state, push, ints)

    push, back = pl.pallas_call(
        second_kernel,
        out_shape=(tiles, shape((256, 3, 128), F32)),
        in_specs=[VM, VM, VM, SM],
        out_specs=(VM, VM),
        scratch_shapes=[
            pltpu.VMEM((64, 12, 128), F32),
            pltpu.VMEM((64, 12, 128), F32),
            pltpu.VMEM((4, 10, 8, 128), F32),
            *cell_scratch, *sems, *halo_sems,
        ],
        compiler_params=talking(1),
        name="exchange_impulses",
    )(state, impulse, sums, ints)

    offset, velocity, impulse = pl.pallas_call(
        last_kernel,
        out_shape=(
            shape(particle_offset.shape, F32),
            shape(particle_velocity.shape, F32),
            shape((3, 64, 128), F32),
        ),
        in_specs=[VM, VM, SM, VM, SM],
        out_specs=(VM, VM, VM),
        compiler_params=plain,
        name="finish",
    )(state, push, ints, back, pos)
    return offset, velocity, jnp.transpose(impulse, (1, 0, 2))


def solution(mesh):
    everyone = ("vehicle", "track", "cross")
    in_specs = (
        P(None, ("vehicle", "track"), "cross", None),
        P(None, ("vehicle", "track"), "cross", None),
        P(("vehicle", "track"), "cross"),
        P(everyone, None, None),
        P(everyone, None, None),
        P(everyone, None),
        P(everyone),
    )
    out_specs = (
        P(None, ("vehicle", "track"), "cross", None),
        P(None, ("vehicle", "track"), "cross", None),
        P(everyone, None, None),
    )
    return jax.shard_map(body, mesh=mesh, in_specs=in_specs, out_specs=out_specs, check_vma=False)
```

```python
import functools

import jax
import jax.numpy as jnp
from jax import lax
from jax.experimental import pallas as pl
from jax.experimental.pallas import tpu as pltpu
from jax.sharding import PartitionSpec as P

radius = 0.1
face_radius = 0.15
stiffness = 100.0
damping = 40.0
soften = 0.05
time_step = 0.02
gravity = 9.81
away = 1.0e6

F32 = jnp.float32
BF16 = jnp.bfloat16
MESH = pl.DeviceIdType.MESH
VM = pl.BlockSpec(memory_space=pltpu.VMEM)
SM = pl.BlockSpec(memory_space=pltpu.SMEM)
SIDES = [(a, b) for a in (-1, 0, 1) for b in (-1, 0, 1) if (a, b) != (0, 0)]
N_PEERS = 64
COUNTS = 128
PART = 2
WIDTH = 2


def rows():
    return lax.broadcasted_iota(jnp.int32, (8, 128), 0)


def lanes():
    return lax.broadcasted_iota(jnp.int32, (8, 128), 1)


def roll(tile, shift):
    return pltpu.roll(tile, shift, axis=0)


def resting(sign):
    return jnp.where(rows() == 2, sign * away, 0.0)


def scaled(tile, reach):
    row = rows()
    return jnp.where(row < 3, tile, jnp.where(row < 6, (-damping * reach) * tile, 0.0))


def spread(tile):
    return [jnp.broadcast_to(tile[channel : channel + 1], (8, 128)) for channel in range(6)]


def pushes(own, other, reach):
    x, y, z = (own[axis] - other[axis] for axis in range(3))
    square = x * x + (y * y + (z * z + soften * soften))
    inverse = lax.rsqrt(square)
    depth = jnp.maximum(inverse - 1.0 / reach, 0.0)
    closing = (own[3] - other[3]) * x + (own[4] - other[4]) * y + (own[5] - other[5]) * z
    weight = depth * (stiffness * reach + closing * inverse)
    return weight * x, weight * y, weight * z


def across_lanes(sums_ref, cell):
    found = [jnp.sum(sums_ref[cell, axis].T, axis=0, keepdims=True) for axis in range(3)]
    return jnp.concatenate(found + [jnp.zeros((5, 128), F32)], axis=0)


def place():
    track = lax.axis_index("track")
    cross = lax.axis_index("cross")
    return lax.axis_index("vehicle"), track, cross


def peer_at(step, sign):
    _, track, cross = place()
    dz, rest = lax.rem(step, 8), lax.div(step, 8)
    dx, dc = lax.rem(rest, 4), lax.div(rest, 4)
    x = lax.rem(lax.div(track, 4) + 4 + sign * dx, 4)
    z = lax.rem(cross * 2 + lax.rem(lax.div(track, 2), 2) + 8 + sign * dz, 8)
    core = lax.rem(lax.rem(track, 2) + dc, 2)
    return x * 4 + lax.rem(z, 2) * 2 + core, lax.div(z, 2)


def neighbour(side):
    vehicle, track, cross = place()
    row = lax.rem(vehicle * 16 + track + 64 + side[0], 64)
    return lax.div(row, 16), lax.rem(row, 16), lax.rem(cross + 4 + side[1], 4)


def greet():
    vehicle = lax.axis_index("vehicle")
    barrier = pltpu.get_barrier_semaphore()

    def one(step, carry):
        track, cross = peer_at(step, 1)
        pl.semaphore_signal(
            barrier, inc=1, device_id=(vehicle, track, cross), device_id_type=MESH
        )
        return carry

    for side in SIDES:
        pl.semaphore_signal(barrier, inc=1, device_id=neighbour(side), device_id_type=MESH)
    lax.fori_loop(1, N_PEERS, one, 0)


def meet_all():
    pl.semaphore_wait(pltpu.get_barrier_semaphore(), N_PEERS - 1 + len(SIDES))


def halo_copy(index, ring, send_sem, recv_sem):
    down, right = SIDES[index]
    source_row = {1: pl.ds(2, 1), -1: pl.ds(1, 1), 0: pl.ds(1, 2)}[down]
    target_row = {1: pl.ds(0, 1), -1: pl.ds(3, 1), 0: pl.ds(1, 2)}[down]
    source_column = {1: pl.ds(8, 1), -1: pl.ds(1, 1), 0: pl.ds(1, 8)}[right]
    target_column = {1: pl.ds(0, 1), -1: pl.ds(9, 1), 0: pl.ds(1, 8)}[right]
    return pltpu.make_async_remote_copy(
        src_ref=ring.at[source_row, source_column],
        dst_ref=ring.at[target_row, target_column],
        send_sem=send_sem.at[index],
        recv_sem=recv_sem.at[index],
        device_id=neighbour(SIDES[index]),
        device_id_type=MESH,
    )


def block_copy(step, outgoing, incoming, send_sem, recv_sem):
    vehicle, track, cross = place()
    to_track, to_cross = peer_at(step, 1)
    return pltpu.make_async_remote_copy(
        src_ref=outgoing.at[to_track * 4 + to_cross],
        dst_ref=incoming.at[track * 4 + cross],
        send_sem=send_sem.at[step],
        recv_sem=recv_sem.at[step],
        device_id=(vehicle, to_track, to_cross),
        device_id_type=MESH,
    )


def order(turn):
    return lax.rem(turn * 21, 64)


def parts3(tile):
    high = tile.astype(BF16).astype(F32)
    rest = tile - high
    middle = rest.astype(BF16).astype(F32)
    return high, middle, rest - middle


def set_up_cells(state_ref, count_ref, reach, columns_ref, ring_ref=None):
    line = lax.broadcasted_iota(jnp.int32, (32, 768), 0)
    lane = lax.broadcasted_iota(jnp.int32, (32, 768), 1)
    chosen = (lax.rem(line, 8) == lax.div(lane, 128)) & (line < 24)
    pick = jnp.where(chosen, 1.0, 0.0).astype(BF16)
    for cell in range(16):
        alive = lanes() < count_ref[COUNTS + cell]
        tile = scaled(state_ref[cell], reach)
        own = jnp.where(alive, tile, resting(1.0))
        stack = jnp.concatenate([*parts3(own), jnp.zeros((8, 128), F32)], axis=0)
        wide = jnp.dot(stack.T.astype(BF16), pick, preferred_element_type=F32)
        for channel in range(6):
            columns_ref[cell, channel] = wide[:, 128 * channel : 128 * channel + 128]
        if ring_ref is not None:
            ring_ref[cell // 8 + 1, cell % 8 + 1] = jnp.where(alive, tile, resting(-1.0))


def clear_edges(ring_ref):
    vehicle, track, cross = place()
    line = vehicle * 16 + track
    dead = resting(-1.0)

    @pl.when(line == 0)
    def _():
        for column in range(10):
            ring_ref[0, column] = dead

    @pl.when(line == 63)
    def _():
        for column in range(10):
            ring_ref[3, column] = dead

    @pl.when(cross == 0)
    def _():
        for row in range(4):
            ring_ref[row, 0] = dead

    @pl.when(cross == 3)
    def _():
        for row in range(4):
            ring_ref[row, 9] = dead


def meet_blocks(cell, part, blocks, columns_ref, ring_ref, sums_ref, base_ref):
    for piece in range(PART):
        start = pl.multiple_of(part * (8 * PART) + 8 * piece, 8)
        own = [columns_ref[cell, channel, pl.ds(start, 8), :] for channel in range(6)]
        total = [0.0, 0.0, 0.0]
        for row, column, down, right in blocks:
            other = spread(ring_ref[row, column])
            shifted = [own[0] - down, own[1] - right] + own[2:]
            push = pushes(shifted, other, 2.0 * radius)
            total = [total[axis] + push[axis] for axis in range(3)]
        for axis in range(3):
            total[axis] = total[axis] + base_ref[cell, axis, pl.ds(start, 8), :]
            sums_ref[cell, axis, pl.ds(start, 8), :] = total[axis]


def own_pushes(row, column, partners, columns_ref, ring_ref, sums_ref, out_ref, base_ref):
    cell = row * 8 + column

    def one(part, carry):
        back = list(carry)
        for piece in range(PART):
            start = pl.multiple_of(part * (8 * PART) + 8 * piece, 8)
            own = [columns_ref[cell, channel, pl.ds(start, 8), :] for channel in range(6)]
            total = list(pushes(own, spread(ring_ref[row + 1, column + 1]), 2.0 * radius))
            for index, (down, right) in enumerate(partners):
                other = spread(ring_ref[row + 1 + down, column + 1 + right])
                shifted = [own[0] - float(down), own[1] - float(right)] + own[2:]
                push = pushes(shifted, other, 2.0 * radius)
                for axis in range(3):
                    total[axis] = total[axis] + push[axis]
                    back[3 * index + axis] = back[3 * index + axis] - push[axis]
            for axis in range(3):
                if base_ref is not None:
                    total[axis] = total[axis] + base_ref[cell, axis, pl.ds(start, 8), :]
                sums_ref[cell, axis, pl.ds(start, 8), :] = total[axis]
        return tuple(back)

    zeros = tuple(jnp.zeros((8, 128), F32) for _ in range(3 * len(partners)))
    back = lax.fori_loop(0, 16 // PART, one, zeros)
    for index, (down, right) in enumerate(partners):
        lines = [jnp.sum(back[3 * index + axis], axis=0, keepdims=True) for axis in range(3)]
        partner = (row + down) * 8 + column + right
        tile = jnp.concatenate(lines + [jnp.zeros((5, 128), F32)], axis=0)
        out_ref[partner] = out_ref[partner] + tile


def inner_pushes(ring_ref, columns_ref, sums_ref, out_ref, base_ref=None):
    refs = (columns_ref, ring_ref, sums_ref, out_ref, base_ref)
    out_ref[...] = jnp.zeros_like(out_ref)

    def one(column, carry):
        own_pushes(0, column, [(1, 0), (0, 1), (1, 1)], *refs)
        own_pushes(1, column, [(0, 1), (-1, 1)], *refs)
        return carry

    lax.fori_loop(0, 7, one, 0)
    own_pushes(0, 7, [(1, 0)], *refs)
    own_pushes(1, 7, [], *refs)


def outer_pushes(ring_ref, columns_ref, sums_ref, out_ref):
    parts = 16 // PART

    def one(turn, carry):
        cell, part = lax.div(turn, parts), lax.rem(turn, parts)
        row, column = lax.div(cell, 8), lax.rem(cell, 8)
        down = (2 * row - 1).astype(F32)
        blocks = [(3 * row, column + 1 + right, down, float(right)) for right in (-1, 0, 1)]
        meet_blocks(cell, part, blocks, columns_ref, ring_ref, sums_ref, sums_ref)
        return carry

    lax.fori_loop(0, 16 * parts, one, 0)

    def side(turn, carry):
        which, part = lax.div(turn, parts), lax.rem(turn, parts)
        row, end = lax.div(which, 2), lax.rem(which, 2)
        right = (2 * end - 1).astype(F32)
        blocks = [(other + 1, 9 * end, (other - row).astype(F32), right) for other in range(2)]
        meet_blocks(row * 8 + 7 * end, part, blocks, columns_ref, ring_ref, sums_ref, sums_ref)
        return carry

    lax.fori_loop(0, 4 * parts, side, 0)

    def gather(cell, carry):
        out_ref[cell] = out_ref[cell] + across_lanes(sums_ref, cell)
        return carry

    lax.fori_loop(0, 16, gather, 0, unroll=4)


def pack_kernel(parts_ref, blocks_ref, ints_ref, state_ref, send_ref, pos_ref, used):
    send_ref[:, 24:25, :] = jnp.full((N_PEERS, 1, 128), -1.0, F32)

    def clear(index, carry):
        used[index] = 0
        return carry

    lax.fori_loop(0, N_PEERS, clear, 0, unroll=8)
    for row in range(2):
        for column in range(8):
            cell = row * 8 + column
            for channel in range(6):
                state_ref[cell, channel : channel + 1, :] = parts_ref[channel, row, column : column + 1, :]
            state_ref[cell, 6:8, :] = jnp.zeros((2, 128), F32)
    lane = lax.broadcasted_iota(jnp.int32, (1, 128), 1)

    def one(block, carry):
        target = ints_ref[block]
        slot = used[target]
        used[target] = slot + 1
        pos_ref[block] = target * 4 + slot
        touched = ints_ref[N_PEERS + block].astype(F32)
        send_ref[target, 24:25, :] = jnp.where(lane == slot, touched, send_ref[target, 24:25, :])
        for channel in range(6):
            send_ref[target, pl.ds(slot * 6 + channel, 1), :] = blocks_ref[channel, pl.ds(block, 1), :]
        return carry

    lax.fori_loop(0, N_PEERS, one, 0, unroll=4)


def first_kernel(
    state_ref, send_ref, count_ref,
    faces_ref, cells_ref, push_ref,
    recv, ring, columns, sums,
    data_out, data_in, halo_out, halo_in,
):
    _, track, cross = place()
    me = track * 4 + cross
    greet()
    set_up_cells(state_ref, count_ref, 2.0 * radius, columns, ring)
    meet_all()
    for index in range(8):
        halo_copy(index, ring, halo_out, halo_in).start()

    def start(turn, carry):
        step = order(turn)
        block_copy(step, send_ref, recv, data_out, data_in).start()
        return carry

    lax.fori_loop(1, N_PEERS, start, 0)
    inner_pushes(ring, columns, sums, push_ref)
    for index in range(8):
        halo_copy(index, ring, halo_out, halo_in).wait()
    clear_edges(ring)
    outer_pushes(ring, columns, sums, push_ref)
    for slot in range(4):
        faces_ref[me * 4 + slot, 0:6, :] = send_ref[me, slot * 6 : slot * 6 + 6, :]
    faces_ref[256] = resting(-1.0)
    cells_ref[me] = send_ref[me, 24:25, :]

    def finish(turn, carry):
        step = order(turn)
        block_copy(step, send_ref, recv, data_out, data_in).wait()
        from_track, from_cross = peer_at(step, -1)
        source = from_track * 4 + from_cross
        for slot in range(4):
            faces_ref[source * 4 + slot, 0:6, :] = recv[source, slot * 6 : slot * 6 + 6, :]
        cells_ref[source] = recv[source, 24:25, :]
        return carry

    lax.fori_loop(1, N_PEERS, finish, 0)


def face_kernel(
    faces_ref, cells_ref, state_ref, push_ref, count_ref,
    next_ref, sums, impulse_ref,
    columns, now, filled, listing,
):
    room = 256 + WIDTH
    for cell in range(17):
        filled[cell] = 0

    def enter(index, carry):
        named = cells_ref[lax.div(index, 4), 0, lax.rem(index, 4)].astype(jnp.int32)
        cell = jnp.where(named >= 0, named, 16)
        count = filled[cell]
        listing[cell * room + count] = index
        filled[cell] = count + 1
        return carry

    lax.fori_loop(0, 256, enter, 0, unroll=4)
    for cell in range(16):
        for extra in range(WIDTH - 1):
            listing[cell * room + filled[cell] + extra] = 256
    now[...] = state_ref[...]

    def substep(step, carry):
        moved = time_step * step.astype(F32)
        sums[...] = jnp.zeros_like(sums)
        set_up_cells(now, count_ref, radius + face_radius, columns)

        def contacts(cell, count):
            def one(turn, carry):
                slots = [listing[cell * room + turn * WIDTH + index] for index in range(WIDTH)]
                row = rows()
                others = []
                for slot in slots:
                    tile = faces_ref[slot]
                    tile = tile + jnp.where(row < 3, moved * roll(tile, 5), 0.0)
                    others.append(spread(scaled(tile, radius + face_radius)))
                back = [[0.0, 0.0, 0.0] for _ in slots]
                for part in range(count):
                    span = slice(8 * part, 8 * part + 8)
                    own = [columns[cell, channel, span, :] for channel in range(6)]
                    push = [pushes(own, other, radius + face_radius) for other in others]
                    for axis in range(3):
                        gained = push[0][axis]
                        for other in push[1:]:
                            gained = gained + other[axis]
                        sums[cell, axis, span, :] = sums[cell, axis, span, :] + gained
                        for side in range(WIDTH):
                            back[side][axis] = back[side][axis] + push[side][axis]
                for side in range(WIDTH):
                    lines = [-time_step * jnp.sum(back[side][axis], axis=0, keepdims=True) for axis in range(3)]
                    tile = jnp.concatenate(lines + [jnp.zeros((5, 128), F32)], axis=0)
                    earlier = jnp.where(step == 0, 0.0, impulse_ref[slots[side]])
                    impulse_ref[slots[side]] = earlier + tile
                return carry

            lax.fori_loop(0, lax.div(filled[cell] + WIDTH - 1, WIDTH), one, 0)

        def block(cell, carry):
            spans = lax.div(count_ref[COUNTS + cell] + 7, 8)
            for number in range(4, 17):
                pl.when(spans == number)(functools.partial(contacts, cell, number))
            return carry

        lax.fori_loop(0, 16, block, 0)

        @pl.when(step == 0)
        def _():
            def advance(cell, carry):
                total = push_ref[cell] + across_lanes(sums, cell)
                tile = advanced(now[cell], total, count_ref[COUNTS + cell])
                now[cell] = tile
                next_ref[cell] = tile
                return carry

            lax.fori_loop(0, 16, advance, 0, unroll=4)

        return carry

    lax.fori_loop(0, 2, substep, 0)


def advanced(tile, push, count):
    row = rows()
    force = jnp.where((row < 3) & (lanes() < count), push, 0.0)
    force = force + jnp.where(row == 2, -gravity, 0.0)
    tile = tile + jnp.where((row >= 3) & (row < 6), time_step * roll(force, 3), 0.0)
    return tile + jnp.where(row < 3, time_step * roll(tile, 5), 0.0)


def second_kernel(
    state_ref, impulse_ref, base_ref, count_ref,
    push_ref, back_ref,
    outgoing, recv, ring, columns, sums,
    data_out, data_in, halo_out, halo_in,
):
    _, track, cross = place()
    me = track * 4 + cross
    greet()
    set_up_cells(state_ref, count_ref, 2.0 * radius, columns, ring)
    meet_all()
    for index in range(8):
        halo_copy(index, ring, halo_out, halo_in).start()

    def start(turn, carry):
        step = order(turn)
        to_track, to_cross = peer_at(step, 1)
        target = to_track * 4 + to_cross
        for slot in range(4):
            outgoing[target, slot * 3 : slot * 3 + 3, :] = impulse_ref[target * 4 + slot, 0:3, :]
        block_copy(step, outgoing, recv, data_out, data_in).start()
        return carry

    lax.fori_loop(1, N_PEERS, start, 0)
    inner_pushes(ring, columns, sums, push_ref, base_ref)
    for index in range(8):
        halo_copy(index, ring, halo_out, halo_in).wait()
    clear_edges(ring)
    outer_pushes(ring, columns, sums, push_ref)
    for slot in range(4):
        back_ref[me * 4 + slot] = impulse_ref[me * 4 + slot, 0:3, :]

    def finish(turn, carry):
        step = order(turn)
        block_copy(step, outgoing, recv, data_out, data_in).wait()
        from_track, from_cross = peer_at(step, -1)
        source = from_track * 4 + from_cross
        for slot in range(4):
            back_ref[source * 4 + slot] = recv[source, slot * 3 : slot * 3 + 3, :]
        return carry

    lax.fori_loop(1, N_PEERS, finish, 0)


def last_kernel(state_ref, push_ref, count_ref, back_ref, pos_ref, offset_ref, velocity_ref, impulse_ref):
    for row in range(2):
        for column in range(8):
            cell = row * 8 + column
            tile = advanced(state_ref[cell], push_ref[cell], count_ref[COUNTS + cell])
            for channel in range(3):
                offset_ref[channel, row, column : column + 1, :] = tile[channel : channel + 1]
                velocity_ref[channel, row, column : column + 1, :] = tile[channel + 3 : channel + 4]

    def one(block, carry):
        slot = pos_ref[block]
        for axis in range(3):
            impulse_ref[axis, pl.ds(block, 1), :] = back_ref[slot, axis : axis + 1, :]
        return carry

    lax.fori_loop(0, N_PEERS, one, 0, unroll=4)


def body(particle_offset, particle_velocity, cell_count, face_offset, face_velocity, face_route, face_cell):
    shape = jax.ShapeDtypeStruct
    tiles = shape((16, 8, 128), F32)
    limit = 48 * 1024 * 1024
    plain = pltpu.CompilerParams(vmem_limit_bytes=limit)

    def talking(name):
        return pltpu.CompilerParams(
            vmem_limit_bytes=limit, collective_id=name, has_side_effects=True
        )

    parts = jnp.concatenate([particle_offset, particle_velocity], axis=0)
    blocks = jnp.concatenate(
        [jnp.transpose(face_offset, (1, 0, 2)), jnp.transpose(face_velocity, (1, 0, 2))], axis=0
    )
    ints = jnp.concatenate([face_route.reshape(-1), face_cell, cell_count.reshape(-1)])
    state, send, pos = pl.pallas_call(
        pack_kernel,
        out_shape=(tiles, shape((64, 25, 128), F32), shape((64,), jnp.int32)),
        in_specs=[VM, VM, SM],
        out_specs=(VM, VM, SM),
        scratch_shapes=[pltpu.SMEM((64,), jnp.int32)],
        compiler_params=plain,
        name="pack",
    )(parts, blocks, ints)

    cell_scratch = [
        pltpu.VMEM((16, 6, 128, 128), F32),
        pltpu.VMEM((16, 3, 128, 128), F32),
    ]
    sems = [pltpu.SemaphoreType.DMA((64,))] * 2
    halo_sems = [pltpu.SemaphoreType.DMA((8,))] * 2
    faces, cells, push = pl.pallas_call(
        first_kernel,
        out_shape=(shape((257, 8, 128), F32), shape((64, 1, 128), F32), tiles),
        in_specs=[VM, VM, SM],
        out_specs=(VM, VM, VM),
        scratch_shapes=[
            pltpu.VMEM((64, 25, 128), F32),
            pltpu.VMEM((4, 10, 8, 128), F32),
            *cell_scratch, *sems, *halo_sems,
        ],
        compiler_params=talking(0),
        name="exchange_faces",
    )(state, send, ints)

    state, sums, impulse = pl.pallas_call(
        face_kernel,
        out_shape=(tiles, shape((16, 3, 128, 128), F32), shape((257, 8, 128), F32)),
        in_specs=[VM, SM, VM, VM, SM],
        out_specs=(VM, VM, VM),
        scratch_shapes=[
            cell_scratch[0],
            pltpu.VMEM((16, 8, 128), F32),
            pltpu.SMEM((17,), jnp.int32),
            pltpu.SMEM((17 * (256 + WIDTH),), jnp.int32),
        ],
        compiler_params=plain,
        name="faces",
    )(faces, cells, state, push, ints)

    push, back = pl.pallas_call(
        second_kernel,
        out_shape=(tiles, shape((256, 3, 128), F32)),
        in_specs=[VM, VM, VM, SM],
        out_specs=(VM, VM),
        scratch_shapes=[
            pltpu.VMEM((64, 12, 128), F32),
            pltpu.VMEM((64, 12, 128), F32),
            pltpu.VMEM((4, 10, 8, 128), F32),
            *cell_scratch, *sems, *halo_sems,
        ],
        compiler_params=talking(1),
        name="exchange_impulses",
    )(state, impulse, sums, ints)

    offset, velocity, impulse = pl.pallas_call(
        last_kernel,
        out_shape=(
            shape(particle_offset.shape, F32),
            shape(particle_velocity.shape, F32),
            shape((3, 64, 128), F32),
        ),
        in_specs=[VM, VM, SM, VM, SM],
        out_specs=(VM, VM, VM),
        compiler_params=plain,
        name="finish",
    )(state, push, ints, back, pos)
    return offset, velocity, jnp.transpose(impulse, (1, 0, 2))


def solution(mesh):
    everyone = ("vehicle", "track", "cross")
    in_specs = (
        P(None, ("vehicle", "track"), "cross", None),
        P(None, ("vehicle", "track"), "cross", None),
        P(("vehicle", "track"), "cross"),
        P(everyone, None, None),
        P(everyone, None, None),
        P(everyone, None),
        P(everyone),
    )
    out_specs = (
        P(None, ("vehicle", "track"), "cross", None),
        P(None, ("vehicle", "track"), "cross", None),
        P(everyone, None, None),
    )
    return jax.shard_map(body, mesh=mesh, in_specs=in_specs, out_specs=out_specs, check_vma=False)
```

```python
import functools

import jax
import jax.numpy as jnp
from jax import lax
from jax.experimental import pallas as pl
from jax.experimental.pallas import tpu as pltpu
from jax.sharding import PartitionSpec as P

radius = 0.1
face_radius = 0.15
stiffness = 100.0
damping = 40.0
soften = 0.05
time_step = 0.02
gravity = 9.81
away = 1.0e6

F32 = jnp.float32
BF16 = jnp.bfloat16
MESH = pl.DeviceIdType.MESH
VM = pl.BlockSpec(memory_space=pltpu.VMEM)
SM = pl.BlockSpec(memory_space=pltpu.SMEM)
SIDES = [(a, b) for a in (-1, 0, 1) for b in (-1, 0, 1) if (a, b) != (0, 0)]
N_PEERS = 64
COUNTS = 128
PART = 4
WIDTH = 2


def rows():
    return lax.broadcasted_iota(jnp.int32, (8, 128), 0)


def lanes():
    return lax.broadcasted_iota(jnp.int32, (8, 128), 1)


def roll(tile, shift):
    return pltpu.roll(tile, shift, axis=0)


def resting(sign):
    return jnp.where(rows() == 2, sign * away, 0.0)


def scaled(tile, reach):
    row = rows()
    return jnp.where(row < 3, tile, jnp.where(row < 6, (-damping * reach) * tile, 0.0))


def spread(tile):
    return [jnp.broadcast_to(tile[channel : channel + 1], (8, 128)) for channel in range(6)]


def pushes(own, other, reach):
    x, y, z = (own[axis] - other[axis] for axis in range(3))
    square = x * x + (y * y + (z * z + soften * soften))
    inverse = lax.rsqrt(square)
    depth = jnp.maximum(inverse - 1.0 / reach, 0.0)
    closing = (own[3] - other[3]) * x + (own[4] - other[4]) * y + (own[5] - other[5]) * z
    weight = depth * (stiffness * reach + closing * inverse)
    return weight * x, weight * y, weight * z


def across_lanes(sums_ref, cell):
    found = [jnp.sum(sums_ref[cell, axis].T, axis=0, keepdims=True) for axis in range(3)]
    return jnp.concatenate(found + [jnp.zeros((5, 128), F32)], axis=0)


def place():
    track = lax.axis_index("track")
    cross = lax.axis_index("cross")
    return lax.axis_index("vehicle"), track, cross


def peer_at(step, sign):
    _, track, cross = place()
    dz, rest = lax.rem(step, 8), lax.div(step, 8)
    dx, dc = lax.rem(rest, 4), lax.div(rest, 4)
    x = lax.rem(lax.div(track, 4) + 4 + sign * dx, 4)
    z = lax.rem(cross * 2 + lax.rem(lax.div(track, 2), 2) + 8 + sign * dz, 8)
    core = lax.rem(lax.rem(track, 2) + dc, 2)
    return x * 4 + lax.rem(z, 2) * 2 + core, lax.div(z, 2)


def neighbour(side):
    vehicle, track, cross = place()
    row = lax.rem(vehicle * 16 + track + 64 + side[0], 64)
    return lax.div(row, 16), lax.rem(row, 16), lax.rem(cross + 4 + side[1], 4)


def greet():
    vehicle = lax.axis_index("vehicle")
    barrier = pltpu.get_barrier_semaphore()

    def one(step, carry):
        track, cross = peer_at(step, 1)
        pl.semaphore_signal(
            barrier, inc=1, device_id=(vehicle, track, cross), device_id_type=MESH
        )
        return carry

    for side in SIDES:
        pl.semaphore_signal(barrier, inc=1, device_id=neighbour(side), device_id_type=MESH)
    lax.fori_loop(1, N_PEERS, one, 0)


def meet_all():
    pl.semaphore_wait(pltpu.get_barrier_semaphore(), N_PEERS - 1 + len(SIDES))


def halo_copy(index, ring, send_sem, recv_sem):
    down, right = SIDES[index]
    source_row = {1: pl.ds(2, 1), -1: pl.ds(1, 1), 0: pl.ds(1, 2)}[down]
    target_row = {1: pl.ds(0, 1), -1: pl.ds(3, 1), 0: pl.ds(1, 2)}[down]
    source_column = {1: pl.ds(8, 1), -1: pl.ds(1, 1), 0: pl.ds(1, 8)}[right]
    target_column = {1: pl.ds(0, 1), -1: pl.ds(9, 1), 0: pl.ds(1, 8)}[right]
    return pltpu.make_async_remote_copy(
        src_ref=ring.at[source_row, source_column],
        dst_ref=ring.at[target_row, target_column],
        send_sem=send_sem.at[index],
        recv_sem=recv_sem.at[index],
        device_id=neighbour(SIDES[index]),
        device_id_type=MESH,
    )


def block_copy(step, outgoing, incoming, send_sem, recv_sem):
    vehicle, track, cross = place()
    to_track, to_cross = peer_at(step, 1)
    return pltpu.make_async_remote_copy(
        src_ref=outgoing.at[to_track * 4 + to_cross],
        dst_ref=incoming.at[track * 4 + cross],
        send_sem=send_sem.at[step],
        recv_sem=recv_sem.at[step],
        device_id=(vehicle, to_track, to_cross),
        device_id_type=MESH,
    )


def order(turn):
    return lax.rem(turn * 21, 64)


def parts3(tile):
    high = tile.astype(BF16).astype(F32)
    rest = tile - high
    middle = rest.astype(BF16).astype(F32)
    return high, middle, rest - middle


def set_up_cells(state_ref, count_ref, reach, columns_ref, ring_ref=None):
    line = lax.broadcasted_iota(jnp.int32, (32, 768), 0)
    lane = lax.broadcasted_iota(jnp.int32, (32, 768), 1)
    chosen = (lax.rem(line, 8) == lax.div(lane, 128)) & (line < 24)
    pick = jnp.where(chosen, 1.0, 0.0).astype(BF16)
    for cell in range(16):
        alive = lanes() < count_ref[COUNTS + cell]
        tile = scaled(state_ref[cell], reach)
        own = jnp.where(alive, tile, resting(1.0))
        stack = jnp.concatenate([*parts3(own), jnp.zeros((8, 128), F32)], axis=0)
        wide = jnp.dot(stack.T.astype(BF16), pick, preferred_element_type=F32)
        for channel in range(6):
            columns_ref[cell, channel] = wide[:, 128 * channel : 128 * channel + 128]
        if ring_ref is not None:
            ring_ref[cell // 8 + 1, cell % 8 + 1] = jnp.where(alive, tile, resting(-1.0))


def clear_edges(ring_ref):
    vehicle, track, cross = place()
    line = vehicle * 16 + track
    dead = resting(-1.0)

    @pl.when(line == 0)
    def _():
        for column in range(10):
            ring_ref[0, column] = dead

    @pl.when(line == 63)
    def _():
        for column in range(10):
            ring_ref[3, column] = dead

    @pl.when(cross == 0)
    def _():
        for row in range(4):
            ring_ref[row, 0] = dead

    @pl.when(cross == 3)
    def _():
        for row in range(4):
            ring_ref[row, 9] = dead


def meet_blocks(cell, part, blocks, columns_ref, ring_ref, sums_ref, base_ref):
    for piece in range(PART):
        start = pl.multiple_of(part * (8 * PART) + 8 * piece, 8)
        own = [columns_ref[cell, channel, pl.ds(start, 8), :] for channel in range(6)]
        total = [0.0, 0.0, 0.0]
        for row, column, down, right in blocks:
            other = spread(ring_ref[row, column])
            shifted = [own[0] - down, own[1] - right] + own[2:]
            push = pushes(shifted, other, 2.0 * radius)
            total = [total[axis] + push[axis] for axis in range(3)]
        for axis in range(3):
            total[axis] = total[axis] + base_ref[cell, axis, pl.ds(start, 8), :]
            sums_ref[cell, axis, pl.ds(start, 8), :] = total[axis]


def own_pushes(row, column, partners, columns_ref, ring_ref, sums_ref, out_ref, base_ref):
    cell = row * 8 + column

    def one(part, carry):
        back = list(carry)
        for piece in range(PART):
            start = pl.multiple_of(part * (8 * PART) + 8 * piece, 8)
            own = [columns_ref[cell, channel, pl.ds(start, 8), :] for channel in range(6)]
            total = list(pushes(own, spread(ring_ref[row + 1, column + 1]), 2.0 * radius))
            for index, (down, right) in enumerate(partners):
                other = spread(ring_ref[row + 1 + down, column + 1 + right])
                shifted = [own[0] - float(down), own[1] - float(right)] + own[2:]
                push = pushes(shifted, other, 2.0 * radius)
                for axis in range(3):
                    total[axis] = total[axis] + push[axis]
                    back[3 * index + axis] = back[3 * index + axis] - push[axis]
            for axis in range(3):
                if base_ref is not None:
                    total[axis] = total[axis] + base_ref[cell, axis, pl.ds(start, 8), :]
                sums_ref[cell, axis, pl.ds(start, 8), :] = total[axis]
        return tuple(back)

    zeros = tuple(jnp.zeros((8, 128), F32) for _ in range(3 * len(partners)))
    back = lax.fori_loop(0, 16 // PART, one, zeros)
    for index, (down, right) in enumerate(partners):
        lines = [jnp.sum(back[3 * index + axis], axis=0, keepdims=True) for axis in range(3)]
        partner = (row + down) * 8 + column + right
        tile = jnp.concatenate(lines + [jnp.zeros((5, 128), F32)], axis=0)
        out_ref[partner] = out_ref[partner] + tile


def inner_pushes(ring_ref, columns_ref, sums_ref, out_ref, base_ref=None):
    refs = (columns_ref, ring_ref, sums_ref, out_ref, base_ref)
    out_ref[...] = jnp.zeros_like(out_ref)

    def one(column, carry):
        own_pushes(0, column, [(1, 0), (0, 1), (1, 1)], *refs)
        own_pushes(1, column, [(0, 1), (-1, 1)], *refs)
        return carry

    lax.fori_loop(0, 7, one, 0)
    own_pushes(0, 7, [(1, 0)], *refs)
    own_pushes(1, 7, [], *refs)


def outer_pushes(ring_ref, columns_ref, sums_ref, out_ref):
    parts = 16 // PART

    def one(turn, carry):
        cell, part = lax.div(turn, parts), lax.rem(turn, parts)
        row, column = lax.div(cell, 8), lax.rem(cell, 8)
        down = (2 * row - 1).astype(F32)
        blocks = [(3 * row, column + 1 + right, down, float(right)) for right in (-1, 0, 1)]
        meet_blocks(cell, part, blocks, columns_ref, ring_ref, sums_ref, sums_ref)
        return carry

    lax.fori_loop(0, 16 * parts, one, 0)

    def side(turn, carry):
        which, part = lax.div(turn, parts), lax.rem(turn, parts)
        row, end = lax.div(which, 2), lax.rem(which, 2)
        right = (2 * end - 1).astype(F32)
        blocks = [(other + 1, 9 * end, (other - row).astype(F32), right) for other in range(2)]
        meet_blocks(row * 8 + 7 * end, part, blocks, columns_ref, ring_ref, sums_ref, sums_ref)
        return carry

    lax.fori_loop(0, 4 * parts, side, 0)

    def gather(cell, carry):
        out_ref[cell] = out_ref[cell] + across_lanes(sums_ref, cell)
        return carry

    lax.fori_loop(0, 16, gather, 0, unroll=4)


def pack_kernel(parts_ref, blocks_ref, ints_ref, state_ref, send_ref, pos_ref, used):
    send_ref[:, 24:25, :] = jnp.full((N_PEERS, 1, 128), -1.0, F32)

    def clear(index, carry):
        used[index] = 0
        return carry

    lax.fori_loop(0, N_PEERS, clear, 0, unroll=8)
    for row in range(2):
        for column in range(8):
            cell = row * 8 + column
            for channel in range(6):
                state_ref[cell, channel : channel + 1, :] = parts_ref[channel, row, column : column + 1, :]
            state_ref[cell, 6:8, :] = jnp.zeros((2, 128), F32)
    lane = lax.broadcasted_iota(jnp.int32, (1, 128), 1)

    def one(block, carry):
        target = ints_ref[block]
        slot = used[target]
        used[target] = slot + 1
        pos_ref[block] = target * 4 + slot
        touched = ints_ref[N_PEERS + block].astype(F32)
        send_ref[target, 24:25, :] = jnp.where(lane == slot, touched, send_ref[target, 24:25, :])
        for channel in range(6):
            send_ref[target, pl.ds(slot * 6 + channel, 1), :] = blocks_ref[channel, pl.ds(block, 1), :]
        return carry

    lax.fori_loop(0, N_PEERS, one, 0, unroll=4)


def first_kernel(
    state_ref, send_ref, count_ref,
    faces_ref, cells_ref, push_ref,
    recv, ring, columns, sums,
    data_out, data_in, halo_out, halo_in,
):
    _, track, cross = place()
    me = track * 4 + cross
    greet()
    set_up_cells(state_ref, count_ref, 2.0 * radius, columns, ring)
    meet_all()
    for index in range(8):
        halo_copy(index, ring, halo_out, halo_in).start()

    def start(turn, carry):
        step = order(turn)
        block_copy(step, send_ref, recv, data_out, data_in).start()
        return carry

    lax.fori_loop(1, N_PEERS, start, 0)
    inner_pushes(ring, columns, sums, push_ref)
    for index in range(8):
        halo_copy(index, ring, halo_out, halo_in).wait()
    clear_edges(ring)
    outer_pushes(ring, columns, sums, push_ref)
    for slot in range(4):
        faces_ref[me * 4 + slot, 0:6, :] = send_ref[me, slot * 6 : slot * 6 + 6, :]
    faces_ref[256] = resting(-1.0)
    cells_ref[me] = send_ref[me, 24:25, :]

    def finish(turn, carry):
        step = order(turn)
        block_copy(step, send_ref, recv, data_out, data_in).wait()
        from_track, from_cross = peer_at(step, -1)
        source = from_track * 4 + from_cross
        for slot in range(4):
            faces_ref[source * 4 + slot, 0:6, :] = recv[source, slot * 6 : slot * 6 + 6, :]
        cells_ref[source] = recv[source, 24:25, :]
        return carry

    lax.fori_loop(1, N_PEERS, finish, 0)


def face_kernel(
    faces_ref, cells_ref, state_ref, push_ref, count_ref,
    next_ref, sums, impulse_ref,
    columns, now, filled, listing,
):
    room = 256 + WIDTH
    for cell in range(17):
        filled[cell] = 0

    def enter(index, carry):
        named = cells_ref[lax.div(index, 4), 0, lax.rem(index, 4)].astype(jnp.int32)
        cell = jnp.where(named >= 0, named, 16)
        count = filled[cell]
        listing[cell * room + count] = index
        filled[cell] = count + 1
        return carry

    lax.fori_loop(0, 256, enter, 0, unroll=16)
    for cell in range(16):
        for extra in range(WIDTH - 1):
            listing[cell * room + filled[cell] + extra] = 256
    now[...] = state_ref[...]

    def substep(step, carry):
        moved = time_step * step.astype(F32)
        sums[...] = jnp.zeros_like(sums)
        set_up_cells(now, count_ref, radius + face_radius, columns)

        def contacts(cell, count):
            def one(turn, carry):
                slots = [listing[cell * room + turn * WIDTH + index] for index in range(WIDTH)]
                row = rows()
                others = []
                for slot in slots:
                    tile = faces_ref[slot]
                    tile = tile + jnp.where(row < 3, moved * roll(tile, 5), 0.0)
                    others.append(spread(scaled(tile, radius + face_radius)))
                back = [[0.0, 0.0, 0.0] for _ in slots]
                for part in range(count):
                    span = slice(8 * part, 8 * part + 8)
                    own = [columns[cell, channel, span, :] for channel in range(6)]
                    push = [pushes(own, other, radius + face_radius) for other in others]
                    for axis in range(3):
                        gained = push[0][axis]
                        for other in push[1:]:
                            gained = gained + other[axis]
                        sums[cell, axis, span, :] = sums[cell, axis, span, :] + gained
                        for side in range(WIDTH):
                            back[side][axis] = back[side][axis] + push[side][axis]
                for side in range(WIDTH):
                    lines = [-time_step * jnp.sum(back[side][axis], axis=0, keepdims=True) for axis in range(3)]
                    tile = jnp.concatenate(lines + [jnp.zeros((5, 128), F32)], axis=0)
                    earlier = jnp.where(step == 0, 0.0, impulse_ref[slots[side]])
                    impulse_ref[slots[side]] = earlier + tile
                return carry

            lax.fori_loop(0, lax.div(filled[cell] + WIDTH - 1, WIDTH), one, 0)

        def block(cell, carry):
            spans = lax.div(count_ref[COUNTS + cell] + 7, 8)
            for number in range(4, 17):
                pl.when(spans == number)(functools.partial(contacts, cell, number))
            return carry

        lax.fori_loop(0, 16, block, 0)

        @pl.when(step == 0)
        def _():
            def advance(cell, carry):
                total = push_ref[cell] + across_lanes(sums, cell)
                tile = advanced(now[cell], total, count_ref[COUNTS + cell])
                now[cell] = tile
                next_ref[cell] = tile
                return carry

            lax.fori_loop(0, 16, advance, 0, unroll=4)

        return carry

    lax.fori_loop(0, 2, substep, 0)


def advanced(tile, push, count):
    row = rows()
    force = jnp.where((row < 3) & (lanes() < count), push, 0.0)
    force = force + jnp.where(row == 2, -gravity, 0.0)
    tile = tile + jnp.where((row >= 3) & (row < 6), time_step * roll(force, 3), 0.0)
    return tile + jnp.where(row < 3, time_step * roll(tile, 5), 0.0)


def second_kernel(
    state_ref, impulse_ref, base_ref, count_ref,
    push_ref, back_ref,
    outgoing, recv, ring, columns, sums,
    data_out, data_in, halo_out, halo_in,
):
    _, track, cross = place()
    me = track * 4 + cross
    greet()
    set_up_cells(state_ref, count_ref, 2.0 * radius, columns, ring)
    meet_all()
    for index in range(8):
        halo_copy(index, ring, halo_out, halo_in).start()

    def start(turn, carry):
        step = order(turn)
        to_track, to_cross = peer_at(step, 1)
        target = to_track * 4 + to_cross
        for slot in range(4):
            outgoing[target, slot * 3 : slot * 3 + 3, :] = impulse_ref[target * 4 + slot, 0:3, :]
        block_copy(step, outgoing, recv, data_out, data_in).start()
        return carry

    lax.fori_loop(1, N_PEERS, start, 0)
    inner_pushes(ring, columns, sums, push_ref, base_ref)
    for index in range(8):
        halo_copy(index, ring, halo_out, halo_in).wait()
    clear_edges(ring)
    outer_pushes(ring, columns, sums, push_ref)
    for slot in range(4):
        back_ref[me * 4 + slot] = impulse_ref[me * 4 + slot, 0:3, :]

    def finish(turn, carry):
        step = order(turn)
        block_copy(step, outgoing, recv, data_out, data_in).wait()
        from_track, from_cross = peer_at(step, -1)
        source = from_track * 4 + from_cross
        for slot in range(4):
            back_ref[source * 4 + slot] = recv[source, slot * 3 : slot * 3 + 3, :]
        return carry

    lax.fori_loop(1, N_PEERS, finish, 0)


def last_kernel(state_ref, push_ref, count_ref, back_ref, pos_ref, offset_ref, velocity_ref, impulse_ref):
    for row in range(2):
        for column in range(8):
            cell = row * 8 + column
            tile = advanced(state_ref[cell], push_ref[cell], count_ref[COUNTS + cell])
            for channel in range(3):
                offset_ref[channel, row, column : column + 1, :] = tile[channel : channel + 1]
                velocity_ref[channel, row, column : column + 1, :] = tile[channel + 3 : channel + 4]

    def one(block, carry):
        slot = pos_ref[block]
        for axis in range(3):
            impulse_ref[axis, pl.ds(block, 1), :] = back_ref[slot, axis : axis + 1, :]
        return carry

    lax.fori_loop(0, N_PEERS, one, 0, unroll=4)


def body(particle_offset, particle_velocity, cell_count, face_offset, face_velocity, face_route, face_cell):
    shape = jax.ShapeDtypeStruct
    tiles = shape((16, 8, 128), F32)
    limit = 48 * 1024 * 1024
    plain = pltpu.CompilerParams(vmem_limit_bytes=limit)

    def talking(name):
        return pltpu.CompilerParams(
            vmem_limit_bytes=limit, collective_id=name, has_side_effects=True
        )

    parts = jnp.concatenate([particle_offset, particle_velocity], axis=0)
    blocks = jnp.concatenate(
        [jnp.transpose(face_offset, (1, 0, 2)), jnp.transpose(face_velocity, (1, 0, 2))], axis=0
    )
    ints = jnp.concatenate([face_route.reshape(-1), face_cell, cell_count.reshape(-1)])
    state, send, pos = pl.pallas_call(
        pack_kernel,
        out_shape=(tiles, shape((64, 25, 128), F32), shape((64,), jnp.int32)),
        in_specs=[VM, VM, SM],
        out_specs=(VM, VM, SM),
        scratch_shapes=[pltpu.SMEM((64,), jnp.int32)],
        compiler_params=plain,
        name="pack",
    )(parts, blocks, ints)

    cell_scratch = [
        pltpu.VMEM((16, 6, 128, 128), F32),
        pltpu.VMEM((16, 3, 128, 128), F32),
    ]
    sems = [pltpu.SemaphoreType.DMA((64,))] * 2
    halo_sems = [pltpu.SemaphoreType.DMA((8,))] * 2
    faces, cells, push = pl.pallas_call(
        first_kernel,
        out_shape=(shape((257, 8, 128), F32), shape((64, 1, 128), F32), tiles),
        in_specs=[VM, VM, SM],
        out_specs=(VM, VM, VM),
        scratch_shapes=[
            pltpu.VMEM((64, 25, 128), F32),
            pltpu.VMEM((4, 10, 8, 128), F32),
            *cell_scratch, *sems, *halo_sems,
        ],
        compiler_params=talking(0),
        name="exchange_faces",
    )(state, send, ints)

    state, sums, impulse = pl.pallas_call(
        face_kernel,
        out_shape=(tiles, shape((16, 3, 128, 128), F32), shape((257, 8, 128), F32)),
        in_specs=[VM, SM, VM, VM, SM],
        out_specs=(VM, VM, VM),
        scratch_shapes=[
            cell_scratch[0],
            pltpu.VMEM((16, 8, 128), F32),
            pltpu.SMEM((17,), jnp.int32),
            pltpu.SMEM((17 * (256 + WIDTH),), jnp.int32),
        ],
        compiler_params=plain,
        name="faces",
    )(faces, cells, state, push, ints)

    push, back = pl.pallas_call(
        second_kernel,
        out_shape=(tiles, shape((256, 3, 128), F32)),
        in_specs=[VM, VM, VM, SM],
        out_specs=(VM, VM),
        scratch_shapes=[
            pltpu.VMEM((64, 12, 128), F32),
            pltpu.VMEM((64, 12, 128), F32),
            pltpu.VMEM((4, 10, 8, 128), F32),
            *cell_scratch, *sems, *halo_sems,
        ],
        compiler_params=talking(1),
        name="exchange_impulses",
    )(state, impulse, sums, ints)

    offset, velocity, impulse = pl.pallas_call(
        last_kernel,
        out_shape=(
            shape(particle_offset.shape, F32),
            shape(particle_velocity.shape, F32),
            shape((3, 64, 128), F32),
        ),
        in_specs=[VM, VM, SM, VM, SM],
        out_specs=(VM, VM, VM),
        compiler_params=plain,
        name="finish",
    )(state, push, ints, back, pos)
    return offset, velocity, jnp.transpose(impulse, (1, 0, 2))


def solution(mesh):
    everyone = ("vehicle", "track", "cross")
    in_specs = (
        P(None, ("vehicle", "track"), "cross", None),
        P(None, ("vehicle", "track"), "cross", None),
        P(("vehicle", "track"), "cross"),
        P(everyone, None, None),
        P(everyone, None, None),
        P(everyone, None),
        P(everyone),
    )
    out_specs = (
        P(None, ("vehicle", "track"), "cross", None),
        P(None, ("vehicle", "track"), "cross", None),
        P(everyone, None, None),
    )
    return jax.shard_map(body, mesh=mesh, in_specs=in_specs, out_specs=out_specs, check_vma=False)
```

```python
import functools

import jax
import jax.numpy as jnp
from jax import lax
from jax.experimental import pallas as pl
from jax.experimental.pallas import tpu as pltpu
from jax.sharding import PartitionSpec as P

radius = 0.1
face_radius = 0.15
stiffness = 100.0
damping = 40.0
soften = 0.05
time_step = 0.02
gravity = 9.81
away = 1.0e6

F32 = jnp.float32
BF16 = jnp.bfloat16
MESH = pl.DeviceIdType.MESH
VM = pl.BlockSpec(memory_space=pltpu.VMEM)
SM = pl.BlockSpec(memory_space=pltpu.SMEM)
SIDES = [(a, b) for a in (-1, 0, 1) for b in (-1, 0, 1) if (a, b) != (0, 0)]
N_PEERS = 64
COUNTS = 128
PART = 4
WIDTH = 2


def rows():
    return lax.broadcasted_iota(jnp.int32, (8, 128), 0)


def lanes():
    return lax.broadcasted_iota(jnp.int32, (8, 128), 1)


def roll(tile, shift):
    return pltpu.roll(tile, shift, axis=0)


def resting(sign):
    return jnp.where(rows() == 2, sign * away, 0.0)


def scaled(tile, reach):
    row = rows()
    return jnp.where(row < 3, tile, jnp.where(row < 6, (-damping * reach) * tile, 0.0))


def spread(tile):
    return [jnp.broadcast_to(tile[channel : channel + 1], (8, 128)) for channel in range(6)]


def pushes(own, other, reach):
    x, y, z = (own[axis] - other[axis] for axis in range(3))
    square = x * x + (y * y + (z * z + soften * soften))
    inverse = lax.rsqrt(square)
    depth = jnp.maximum(inverse - 1.0 / reach, 0.0)
    closing = (own[3] - other[3]) * x + (own[4] - other[4]) * y + (own[5] - other[5]) * z
    weight = depth * (stiffness * reach + closing * inverse)
    return weight * x, weight * y, weight * z


def across_lanes(sums_ref, cell):
    found = [jnp.sum(sums_ref[cell, axis].T, axis=0, keepdims=True) for axis in range(3)]
    return jnp.concatenate(found + [jnp.zeros((5, 128), F32)], axis=0)


def place():
    track = lax.axis_index("track")
    cross = lax.axis_index("cross")
    return lax.axis_index("vehicle"), track, cross


def peer_at(step, sign):
    _, track, cross = place()
    dz, rest = lax.rem(step, 8), lax.div(step, 8)
    dx, dc = lax.rem(rest, 4), lax.div(rest, 4)
    x = lax.rem(lax.div(track, 4) + 4 + sign * dx, 4)
    z = lax.rem(cross * 2 + lax.rem(lax.div(track, 2), 2) + 8 + sign * dz, 8)
    core = lax.rem(lax.rem(track, 2) + dc, 2)
    return x * 4 + lax.rem(z, 2) * 2 + core, lax.div(z, 2)


def neighbour(side):
    vehicle, track, cross = place()
    row = lax.rem(vehicle * 16 + track + 64 + side[0], 64)
    return lax.div(row, 16), lax.rem(row, 16), lax.rem(cross + 4 + side[1], 4)


def greet():
    vehicle = lax.axis_index("vehicle")
    barrier = pltpu.get_barrier_semaphore()

    def one(step, carry):
        track, cross = peer_at(step, 1)
        pl.semaphore_signal(
            barrier, inc=1, device_id=(vehicle, track, cross), device_id_type=MESH
        )
        return carry

    for side in SIDES:
        pl.semaphore_signal(barrier, inc=1, device_id=neighbour(side), device_id_type=MESH)
    lax.fori_loop(1, N_PEERS, one, 0, unroll=3)


def meet_all():
    pl.semaphore_wait(pltpu.get_barrier_semaphore(), N_PEERS - 1 + len(SIDES))


def halo_copy(index, ring, send_sem, recv_sem):
    down, right = SIDES[index]
    source_row = {1: pl.ds(2, 1), -1: pl.ds(1, 1), 0: pl.ds(1, 2)}[down]
    target_row = {1: pl.ds(0, 1), -1: pl.ds(3, 1), 0: pl.ds(1, 2)}[down]
    source_column = {1: pl.ds(8, 1), -1: pl.ds(1, 1), 0: pl.ds(1, 8)}[right]
    target_column = {1: pl.ds(0, 1), -1: pl.ds(9, 1), 0: pl.ds(1, 8)}[right]
    return pltpu.make_async_remote_copy(
        src_ref=ring.at[source_row, source_column],
        dst_ref=ring.at[target_row, target_column],
        send_sem=send_sem.at[index],
        recv_sem=recv_sem.at[index],
        device_id=neighbour(SIDES[index]),
        device_id_type=MESH,
    )


def block_copy(step, outgoing, incoming, send_sem, recv_sem):
    vehicle, track, cross = place()
    to_track, to_cross = peer_at(step, 1)
    return pltpu.make_async_remote_copy(
        src_ref=outgoing.at[to_track * 4 + to_cross],
        dst_ref=incoming.at[track * 4 + cross],
        send_sem=send_sem.at[step],
        recv_sem=recv_sem.at[step],
        device_id=(vehicle, to_track, to_cross),
        device_id_type=MESH,
    )


def order(turn):
    return lax.rem(turn * 21, 64)


def parts3(tile):
    high = tile.astype(BF16).astype(F32)
    rest = tile - high
    middle = rest.astype(BF16).astype(F32)
    return high, middle, rest - middle


def set_up_cells(state_ref, count_ref, reach, columns_ref, ring_ref=None):
    line = lax.broadcasted_iota(jnp.int32, (32, 768), 0)
    lane = lax.broadcasted_iota(jnp.int32, (32, 768), 1)
    chosen = (lax.rem(line, 8) == lax.div(lane, 128)) & (line < 24)
    pick = jnp.where(chosen, 1.0, 0.0).astype(BF16)
    for cell in range(16):
        alive = lanes() < count_ref[COUNTS + cell]
        tile = scaled(state_ref[cell], reach)
        own = jnp.where(alive, tile, resting(1.0))
        stack = jnp.concatenate([*parts3(own), jnp.zeros((8, 128), F32)], axis=0)
        wide = jnp.dot(stack.T.astype(BF16), pick, preferred_element_type=F32)
        for channel in range(6):
            columns_ref[cell, channel] = wide[:, 128 * channel : 128 * channel + 128]
        if ring_ref is not None:
            ring_ref[cell // 8 + 1, cell % 8 + 1] = jnp.where(alive, tile, resting(-1.0))


def clear_edges(ring_ref):
    vehicle, track, cross = place()
    line = vehicle * 16 + track
    dead = resting(-1.0)

    @pl.when(line == 0)
    def _():
        for column in range(10):
            ring_ref[0, column] = dead

    @pl.when(line == 63)
    def _():
        for column in range(10):
            ring_ref[3, column] = dead

    @pl.when(cross == 0)
    def _():
        for row in range(4):
            ring_ref[row, 0] = dead

    @pl.when(cross == 3)
    def _():
        for row in range(4):
            ring_ref[row, 9] = dead


def meet_blocks(cell, part, blocks, columns_ref, ring_ref, sums_ref, base_ref):
    for piece in range(PART):
        start = pl.multiple_of(part * (8 * PART) + 8 * piece, 8)
        own = [columns_ref[cell, channel, pl.ds(start, 8), :] for channel in range(6)]
        total = [0.0, 0.0, 0.0]
        for row, column, down, right in blocks:
            other = spread(ring_ref[row, column])
            shifted = [own[0] - down, own[1] - right] + own[2:]
            push = pushes(shifted, other, 2.0 * radius)
            total = [total[axis] + push[axis] for axis in range(3)]
        for axis in range(3):
            total[axis] = total[axis] + base_ref[cell, axis, pl.ds(start, 8), :]
            sums_ref[cell, axis, pl.ds(start, 8), :] = total[axis]


def own_pushes(row, column, partners, columns_ref, ring_ref, sums_ref, out_ref, base_ref):
    cell = row * 8 + column

    def one(part, carry):
        back = list(carry)
        for piece in range(PART):
            start = pl.multiple_of(part * (8 * PART) + 8 * piece, 8)
            own = [columns_ref[cell, channel, pl.ds(start, 8), :] for channel in range(6)]
            total = list(pushes(own, spread(ring_ref[row + 1, column + 1]), 2.0 * radius))
            for index, (down, right) in enumerate(partners):
                other = spread(ring_ref[row + 1 + down, column + 1 + right])
                shifted = [own[0] - float(down), own[1] - float(right)] + own[2:]
                push = pushes(shifted, other, 2.0 * radius)
                for axis in range(3):
                    total[axis] = total[axis] + push[axis]
                    back[3 * index + axis] = back[3 * index + axis] - push[axis]
            for axis in range(3):
                if base_ref is not None:
                    total[axis] = total[axis] + base_ref[cell, axis, pl.ds(start, 8), :]
                sums_ref[cell, axis, pl.ds(start, 8), :] = total[axis]
        return tuple(back)

    zeros = tuple(jnp.zeros((8, 128), F32) for _ in range(3 * len(partners)))
    back = lax.fori_loop(0, 16 // PART, one, zeros)
    for index, (down, right) in enumerate(partners):
        lines = [jnp.sum(back[3 * index + axis], axis=0, keepdims=True) for axis in range(3)]
        partner = (row + down) * 8 + column + right
        tile = jnp.concatenate(lines + [jnp.zeros((5, 128), F32)], axis=0)
        out_ref[partner] = out_ref[partner] + tile


def inner_pushes(ring_ref, columns_ref, sums_ref, out_ref, base_ref=None):
    refs = (columns_ref, ring_ref, sums_ref, out_ref, base_ref)
    out_ref[...] = jnp.zeros_like(out_ref)

    def one(column, carry):
        own_pushes(0, column, [(1, 0), (0, 1), (1, 1)], *refs)
        own_pushes(1, column, [(0, 1), (-1, 1)], *refs)
        return carry

    lax.fori_loop(0, 7, one, 0)
    own_pushes(0, 7, [(1, 0)], *refs)
    own_pushes(1, 7, [], *refs)


def outer_pushes(ring_ref, columns_ref, sums_ref, out_ref):
    parts = 16 // PART

    def one(turn, carry):
        cell, part = lax.div(turn, parts), lax.rem(turn, parts)
        row, column = lax.div(cell, 8), lax.rem(cell, 8)
        down = (2 * row - 1).astype(F32)
        blocks = [(3 * row, column + 1 + right, down, float(right)) for right in (-1, 0, 1)]
        meet_blocks(cell, part, blocks, columns_ref, ring_ref, sums_ref, sums_ref)
        return carry

    lax.fori_loop(0, 16 * parts, one, 0)

    def side(turn, carry):
        which, part = lax.div(turn, parts), lax.rem(turn, parts)
        row, end = lax.div(which, 2), lax.rem(which, 2)
        right = (2 * end - 1).astype(F32)
        blocks = [(other + 1, 9 * end, (other - row).astype(F32), right) for other in range(2)]
        meet_blocks(row * 8 + 7 * end, part, blocks, columns_ref, ring_ref, sums_ref, sums_ref)
        return carry

    lax.fori_loop(0, 4 * parts, side, 0)

    def gather(cell, carry):
        out_ref[cell] = out_ref[cell] + across_lanes(sums_ref, cell)
        return carry

    lax.fori_loop(0, 16, gather, 0, unroll=8)


def pack_kernel(parts_ref, blocks_ref, ints_ref, state_ref, send_ref, pos_ref, used):
    send_ref[:, 24:25, :] = jnp.full((N_PEERS, 1, 128), -1.0, F32)

    def clear(index, carry):
        used[index] = 0
        return carry

    lax.fori_loop(0, N_PEERS, clear, 0, unroll=8)
    for row in range(2):
        for column in range(8):
            cell = row * 8 + column
            for channel in range(6):
                state_ref[cell, channel : channel + 1, :] = parts_ref[channel, row, column : column + 1, :]
            state_ref[cell, 6:8, :] = jnp.zeros((2, 128), F32)
    lane = lax.broadcasted_iota(jnp.int32, (1, 128), 1)

    def one(block, carry):
        target = ints_ref[block]
        slot = used[target]
        used[target] = slot + 1
        pos_ref[block] = target * 4 + slot
        touched = ints_ref[N_PEERS + block].astype(F32)
        send_ref[target, 24:25, :] = jnp.where(lane == slot, touched, send_ref[target, 24:25, :])
        for channel in range(6):
            send_ref[target, pl.ds(slot * 6 + channel, 1), :] = blocks_ref[channel, pl.ds(block, 1), :]
        return carry

    lax.fori_loop(0, N_PEERS, one, 0, unroll=4)


def first_kernel(
    state_ref, send_ref, count_ref,
    faces_ref, cells_ref, push_ref,
    recv, ring, columns, sums,
    data_out, data_in, halo_out, halo_in,
):
    _, track, cross = place()
    me = track * 4 + cross
    greet()
    set_up_cells(state_ref, count_ref, 2.0 * radius, columns, ring)
    meet_all()
    for index in range(8):
        halo_copy(index, ring, halo_out, halo_in).start()

    def start(turn, carry):
        step = order(turn)
        block_copy(step, send_ref, recv, data_out, data_in).start()
        return carry

    lax.fori_loop(1, N_PEERS, start, 0, unroll=3)
    inner_pushes(ring, columns, sums, push_ref)
    for index in range(8):
        halo_copy(index, ring, halo_out, halo_in).wait()
    clear_edges(ring)
    outer_pushes(ring, columns, sums, push_ref)
    for slot in range(4):
        faces_ref[me * 4 + slot, 0:6, :] = send_ref[me, slot * 6 : slot * 6 + 6, :]
    faces_ref[256] = resting(-1.0)
    cells_ref[me] = send_ref[me, 24:25, :]

    def finish(turn, carry):
        step = order(turn)
        block_copy(step, send_ref, recv, data_out, data_in).wait()
        from_track, from_cross = peer_at(step, -1)
        source = from_track * 4 + from_cross
        for slot in range(4):
            faces_ref[source * 4 + slot, 0:6, :] = recv[source, slot * 6 : slot * 6 + 6, :]
        cells_ref[source] = recv[source, 24:25, :]
        return carry

    lax.fori_loop(1, N_PEERS, finish, 0, unroll=3)


def face_kernel(
    faces_ref, cells_ref, state_ref, push_ref, count_ref,
    next_ref, sums, impulse_ref,
    columns, now, filled, listing,
):
    room = 256 + WIDTH
    for cell in range(17):
        filled[cell] = 0

    def enter(index, carry):
        named = cells_ref[lax.div(index, 4), 0, lax.rem(index, 4)].astype(jnp.int32)
        cell = jnp.where(named >= 0, named, 16)
        count = filled[cell]
        listing[cell * room + count] = index
        filled[cell] = count + 1
        return carry

    lax.fori_loop(0, 256, enter, 0, unroll=16)
    for cell in range(16):
        for extra in range(WIDTH - 1):
            listing[cell * room + filled[cell] + extra] = 256
    now[...] = state_ref[...]

    def substep(step, carry):
        moved = time_step * step.astype(F32)
        sums[...] = jnp.zeros_like(sums)
        set_up_cells(now, count_ref, radius + face_radius, columns)

        def contacts(cell, count):
            def one(turn, carry):
                slots = [listing[cell * room + turn * WIDTH + index] for index in range(WIDTH)]
                row = rows()
                others = []
                for slot in slots:
                    tile = faces_ref[slot]
                    tile = tile + jnp.where(row < 3, moved * roll(tile, 5), 0.0)
                    others.append(spread(scaled(tile, radius + face_radius)))
                back = [[0.0, 0.0, 0.0] for _ in slots]
                for part in range(count):
                    span = slice(8 * part, 8 * part + 8)
                    own = [columns[cell, channel, span, :] for channel in range(6)]
                    push = [pushes(own, other, radius + face_radius) for other in others]
                    for axis in range(3):
                        gained = push[0][axis]
                        for other in push[1:]:
                            gained = gained + other[axis]
                        sums[cell, axis, span, :] = sums[cell, axis, span, :] + gained
                        for side in range(WIDTH):
                            back[side][axis] = back[side][axis] + push[side][axis]
                for side in range(WIDTH):
                    lines = [-time_step * jnp.sum(back[side][axis], axis=0, keepdims=True) for axis in range(3)]
                    tile = jnp.concatenate(lines + [jnp.zeros((5, 128), F32)], axis=0)
                    earlier = jnp.where(step == 0, 0.0, impulse_ref[slots[side]])
                    impulse_ref[slots[side]] = earlier + tile
                return carry

            lax.fori_loop(0, lax.div(filled[cell] + WIDTH - 1, WIDTH), one, 0)

        def block(cell, carry):
            spans = lax.div(count_ref[COUNTS + cell] + 7, 8)
            for number in range(4, 17):
                pl.when(spans == number)(functools.partial(contacts, cell, number))
            return carry

        lax.fori_loop(0, 16, block, 0)

        @pl.when(step == 0)
        def _():
            def advance(cell, carry):
                total = push_ref[cell] + across_lanes(sums, cell)
                tile = advanced(now[cell], total, count_ref[COUNTS + cell])
                now[cell] = tile
                next_ref[cell] = tile
                return carry

            lax.fori_loop(0, 16, advance, 0, unroll=8)

        return carry

    lax.fori_loop(0, 2, substep, 0)


def advanced(tile, push, count):
    row = rows()
    force = jnp.where((row < 3) & (lanes() < count), push, 0.0)
    force = force + jnp.where(row == 2, -gravity, 0.0)
    tile = tile + jnp.where((row >= 3) & (row < 6), time_step * roll(force, 3), 0.0)
    return tile + jnp.where(row < 3, time_step * roll(tile, 5), 0.0)


def second_kernel(
    state_ref, impulse_ref, base_ref, count_ref,
    push_ref, back_ref,
    outgoing, recv, ring, columns, sums,
    data_out, data_in, halo_out, halo_in,
):
    _, track, cross = place()
    me = track * 4 + cross
    greet()
    set_up_cells(state_ref, count_ref, 2.0 * radius, columns, ring)
    meet_all()
    for index in range(8):
        halo_copy(index, ring, halo_out, halo_in).start()

    def start(turn, carry):
        step = order(turn)
        to_track, to_cross = peer_at(step, 1)
        target = to_track * 4 + to_cross
        for slot in range(4):
            outgoing[target, slot * 3 : slot * 3 + 3, :] = impulse_ref[target * 4 + slot, 0:3, :]
        block_copy(step, outgoing, recv, data_out, data_in).start()
        return carry

    lax.fori_loop(1, N_PEERS, start, 0, unroll=3)
    inner_pushes(ring, columns, sums, push_ref, base_ref)
    for index in range(8):
        halo_copy(index, ring, halo_out, halo_in).wait()
    clear_edges(ring)
    outer_pushes(ring, columns, sums, push_ref)
    for slot in range(4):
        back_ref[me * 4 + slot] = impulse_ref[me * 4 + slot, 0:3, :]

    def finish(turn, carry):
        step = order(turn)
        block_copy(step, outgoing, recv, data_out, data_in).wait()
        from_track, from_cross = peer_at(step, -1)
        source = from_track * 4 + from_cross
        for slot in range(4):
            back_ref[source * 4 + slot] = recv[source, slot * 3 : slot * 3 + 3, :]
        return carry

    lax.fori_loop(1, N_PEERS, finish, 0, unroll=3)


def last_kernel(state_ref, push_ref, count_ref, back_ref, pos_ref, offset_ref, velocity_ref, impulse_ref):
    for row in range(2):
        for column in range(8):
            cell = row * 8 + column
            tile = advanced(state_ref[cell], push_ref[cell], count_ref[COUNTS + cell])
            for channel in range(3):
                offset_ref[channel, row, column : column + 1, :] = tile[channel : channel + 1]
                velocity_ref[channel, row, column : column + 1, :] = tile[channel + 3 : channel + 4]

    def one(block, carry):
        slot = pos_ref[block]
        for axis in range(3):
            impulse_ref[axis, pl.ds(block, 1), :] = back_ref[slot, axis : axis + 1, :]
        return carry

    lax.fori_loop(0, N_PEERS, one, 0, unroll=4)


def body(particle_offset, particle_velocity, cell_count, face_offset, face_velocity, face_route, face_cell):
    shape = jax.ShapeDtypeStruct
    tiles = shape((16, 8, 128), F32)
    limit = 48 * 1024 * 1024
    plain = pltpu.CompilerParams(vmem_limit_bytes=limit)

    def talking(name):
        return pltpu.CompilerParams(
            vmem_limit_bytes=limit, collective_id=name, has_side_effects=True
        )

    parts = jnp.concatenate([particle_offset, particle_velocity], axis=0)
    blocks = jnp.concatenate(
        [jnp.transpose(face_offset, (1, 0, 2)), jnp.transpose(face_velocity, (1, 0, 2))], axis=0
    )
    ints = jnp.concatenate([face_route.reshape(-1), face_cell, cell_count.reshape(-1)])
    state, send, pos = pl.pallas_call(
        pack_kernel,
        out_shape=(tiles, shape((64, 25, 128), F32), shape((64,), jnp.int32)),
        in_specs=[VM, VM, SM],
        out_specs=(VM, VM, SM),
        scratch_shapes=[pltpu.SMEM((64,), jnp.int32)],
        compiler_params=plain,
        name="pack",
    )(parts, blocks, ints)

    cell_scratch = [
        pltpu.VMEM((16, 6, 128, 128), F32),
        pltpu.VMEM((16, 3, 128, 128), F32),
    ]
    sems = [pltpu.SemaphoreType.DMA((64,))] * 2
    halo_sems = [pltpu.SemaphoreType.DMA((8,))] * 2
    faces, cells, push = pl.pallas_call(
        first_kernel,
        out_shape=(shape((257, 8, 128), F32), shape((64, 1, 128), F32), tiles),
        in_specs=[VM, VM, SM],
        out_specs=(VM, VM, VM),
        scratch_shapes=[
            pltpu.VMEM((64, 25, 128), F32),
            pltpu.VMEM((4, 10, 8, 128), F32),
            *cell_scratch, *sems, *halo_sems,
        ],
        compiler_params=talking(0),
        name="exchange_faces",
    )(state, send, ints)

    state, sums, impulse = pl.pallas_call(
        face_kernel,
        out_shape=(tiles, shape((16, 3, 128, 128), F32), shape((257, 8, 128), F32)),
        in_specs=[VM, SM, VM, VM, SM],
        out_specs=(VM, VM, VM),
        scratch_shapes=[
            cell_scratch[0],
            pltpu.VMEM((16, 8, 128), F32),
            pltpu.SMEM((17,), jnp.int32),
            pltpu.SMEM((17 * (256 + WIDTH),), jnp.int32),
        ],
        compiler_params=plain,
        name="faces",
    )(faces, cells, state, push, ints)

    push, back = pl.pallas_call(
        second_kernel,
        out_shape=(tiles, shape((256, 3, 128), F32)),
        in_specs=[VM, VM, VM, SM],
        out_specs=(VM, VM),
        scratch_shapes=[
            pltpu.VMEM((64, 12, 128), F32),
            pltpu.VMEM((64, 12, 128), F32),
            pltpu.VMEM((4, 10, 8, 128), F32),
            *cell_scratch, *sems, *halo_sems,
        ],
        compiler_params=talking(1),
        name="exchange_impulses",
    )(state, impulse, sums, ints)

    offset, velocity, impulse = pl.pallas_call(
        last_kernel,
        out_shape=(
            shape(particle_offset.shape, F32),
            shape(particle_velocity.shape, F32),
            shape((3, 64, 128), F32),
        ),
        in_specs=[VM, VM, SM, VM, SM],
        out_specs=(VM, VM, VM),
        compiler_params=plain,
        name="finish",
    )(state, push, ints, back, pos)
    return offset, velocity, jnp.transpose(impulse, (1, 0, 2))


def solution(mesh):
    everyone = ("vehicle", "track", "cross")
    in_specs = (
        P(None, ("vehicle", "track"), "cross", None),
        P(None, ("vehicle", "track"), "cross", None),
        P(("vehicle", "track"), "cross"),
        P(everyone, None, None),
        P(everyone, None, None),
        P(everyone, None),
        P(everyone),
    )
    out_specs = (
        P(None, ("vehicle", "track"), "cross", None),
        P(None, ("vehicle", "track"), "cross", None),
        P(everyone, None, None),
    )
    return jax.shard_map(body, mesh=mesh, in_specs=in_specs, out_specs=out_specs, check_vma=False)
```
